32 devices in a mesh: seq: 8 (over y, x, core), dp: 4 (over z).
Axes of the slice: x: 2, y: 2, z: 4, core: 2. Of those that a mesh axis runs over, the one named last changes fastest.
Arguments:
- tokens: bfloat16 [16384, 1024], P(('dp', 'seq')), parts along dimension 0, may hold values from -6 to 6
- norm_gain: float32 [1024], replicated, may hold values from 0.25 to 1.75
- query_weight: bfloat16 [1024, 1024], replicated
- key_weight: bfloat16 [1024, 1024], replicated
- value_weight: bfloat16 [1024, 1024], replicated, may hold values from -0.1875 to 0.1875
- out_weight: bfloat16 [1024, 1024], replicated, may hold values from -0.1875 to 0.1875
- random_blocks: int32 [256, 3], P('dp'), parts along dimension 0, may hold values from 0 to 63, as said below
- bucket_id: int32 [1], replicated, may hold values from 0 to 7
- global_positions: int32 [8, 128], replicated, may hold values from 0 to 4095, as said below
Outputs:
- layer_out: bfloat16 [16384, 1024], P(('dp', 'seq')), parts along dimension 0
The draws below stay inside these ranges and needn't reach their ends.
There are 4 independent parts, one for each index of `dp`. The reference program is written for one: setup_inputs(seed, part) draws one part's arguments, and reference() takes and returns one part's arrays. A program takes and returns all parts, laid end to end along the dimension named above; an argument that names none is the same for every part. Nothing has to cross between parts.
Inputs may be any that keep to these rules, and one draw needn't show every extreme that they name: `random_blocks`: each row lists 3 block numbers. For the query blocks of one device (aligned runs of 8 rows) at most 3 of the listed blocks lie within the tokens of any one device, and exactly 3 for some device. A block may be listed more than once. `global_positions`: each row holds 128 distinct positions in rising order.
All inputs are finite; a program needn't handle non-finite values.
Results may differ from the reference program's by a relative error of at most 0.0089.
Values may be sent and summed in bfloat16 or wider, within the bound.
No kernel may reach another device: no remote copies, remote signals or barrier semaphores. Data moves between devices by JAX's collectives and lax.ppermute only.
A program may use at most 128 MiB of HBM per device.

```python
import jax
import jax.numpy as jnp
from jax import lax

D = 1024
HEADS = 16
HDIM = 64
BLOCK = 64
RAND = 3
NGLOB = 128
BUCKETS = 8
TOK_DEV = 512
TOKENS = 4096
NB = 64
N_SEQ = 8


def attention_pair(key):
    base = jax.random.normal(jax.random.fold_in(key, 11), (D, D), jnp.float32) * D ** (-0.5)
    other = jax.random.normal(jax.random.fold_in(key, 12), (D, D), jnp.float32) * D ** (-0.5)
    return (base, other)


def draw_query_weight(key, part):
    return attention_pair(key)[0].astype(jnp.bfloat16)


def draw_key_weight(key, part):
    return attention_pair(key)[1].astype(jnp.bfloat16)


def draw_random_blocks(key, part):
    local_blocks = TOK_DEV // BLOCK
    slots = local_blocks * RAND
    capacity = (slots + N_SEQ - 1) // N_SEQ

    def one_device(device_key):
        order_keys = jax.random.split(jax.random.fold_in(device_key, 1), capacity)
        orders = jax.vmap(lambda order_key: jax.random.permutation(order_key, N_SEQ))(order_keys)
        source = orders.reshape(-1)[:slots]
        source = jax.random.permutation(jax.random.fold_in(device_key, 2), source)
        inner = jax.random.randint(jax.random.fold_in(device_key, 3), (slots,), 0, local_blocks)
        return (source * local_blocks + inner).reshape(local_blocks, RAND)
    device_keys = jax.vmap(lambda index: jax.random.fold_in(key, index))(jnp.arange(N_SEQ))
    return jax.vmap(one_device)(device_keys).reshape(NB, RAND).astype(jnp.int32)


def draw_global_positions(key, part):

    def one_bucket(bucket_key):
        chosen = jax.random.permutation(bucket_key, TOKENS)[:NGLOB]
        return jnp.sort(chosen)
    bucket_keys = jax.vmap(lambda index: jax.random.fold_in(key, index + 100))(jnp.arange(BUCKETS))
    return jax.vmap(one_bucket)(bucket_keys).astype(jnp.int32)


def block_levels(rng, shape, shards, least, largest):
    loudness = 1.0
    for axis_at, shards_of in shards:
        draws = jax.random.uniform(jax.random.fold_in(jax.random.fold_in(rng, 6), axis_at), (shards_of,), jnp.float32, least / len(shards), largest / len(shards))
        loudness = loudness * jnp.repeat(jnp.exp(draws), shape[axis_at] // shards_of).reshape((-1,) + (1,) * (len(shape) - 1 - axis_at))
    return loudness


def normal_values(rng, extent, width, reach, shards=(), kind=jnp.bfloat16):
    level = block_levels(rng, extent, shards, -0.22, 0.18) if shards else 1.0
    array = jax.random.normal(rng, extent, jnp.float32) * width * level
    return jnp.minimum(jnp.maximum(array, -reach), reach).astype(kind)


def setup_inputs(seed: int = 0, part: int = 0) -> dict:
    streams_of = jax.random.split(jax.random.key(seed), 10)
    part_splits = jax.random.split(jax.random.fold_in(streams_of[9], part), 10)
    tokens = normal_values(part_splits[0], (TOKENS, D), 1.0, 6.0, ((0, 8),))
    norm_gain = jnp.clip(1.0 + 0.15 * jax.random.normal(streams_of[1], (D,), jnp.float32), 0.25, 1.75)
    query_weight = draw_query_weight(jax.random.fold_in(streams_of[9], 71), part)
    key_weight = draw_key_weight(jax.random.fold_in(streams_of[9], 71), part)
    value_weight = normal_values(streams_of[4], (D, D), D ** -0.5, 0.1875)
    out_weight = normal_values(streams_of[5], (D, D), D ** -0.5, 0.1875)
    random_blocks = draw_random_blocks(jax.random.fold_in(jax.random.fold_in(streams_of[9], part), 71), part)
    bucket_id = jax.random.randint(streams_of[7], (1,), 0, BUCKETS).astype(jnp.int32)
    global_positions = draw_global_positions(jax.random.fold_in(streams_of[9], 71), part)
    return {"tokens": tokens, "norm_gain": norm_gain, "query_weight": query_weight, "key_weight": key_weight, "value_weight": value_weight, "out_weight": out_weight, "random_blocks": random_blocks, "bucket_id": bucket_id, "global_positions": global_positions}


def layer_norm(tokens, norm_gain):
    values = tokens.astype(jnp.float32)
    center = values - lax.optimization_barrier(jnp.mean(values, axis=-1, keepdims=True))
    spread = lax.optimization_barrier(jnp.mean(center * center, axis=-1, keepdims=True))
    return (center * lax.rsqrt(spread + 1e-05) * norm_gain.astype(jnp.float32)).astype(jnp.bfloat16)

def reference(tokens, norm_gain, query_weight, key_weight, value_weight, out_weight, random_blocks, bucket_id, global_positions):
    normed = layer_norm(tokens, norm_gain)
    queries = jnp.dot(normed, query_weight, preferred_element_type=jnp.float32).astype(jnp.bfloat16)
    key_rows = jnp.dot(normed, key_weight, preferred_element_type=jnp.float32).astype(jnp.bfloat16)
    value_rows = jnp.dot(normed, value_weight, preferred_element_type=jnp.float32).astype(jnp.bfloat16)
    positions = global_positions[bucket_id[0]].astype(jnp.int32)
    scale = HDIM ** (-0.5)
    own = jnp.arange(NB, dtype=jnp.int32)
    window = jnp.stack([(own - 1) % NB, own, (own + 1) % NB], axis=1)
    chosen = jnp.concatenate([window, random_blocks.astype(jnp.int32)], axis=1)
    key_blocks = key_rows.reshape(NB, BLOCK, HEADS, HDIM)
    value_blocks = value_rows.reshape(NB, BLOCK, HEADS, HDIM)
    count = (3 + RAND) * BLOCK
    picked_keys = key_blocks[chosen].reshape(NB, count, HEADS, HDIM)
    picked_values = value_blocks[chosen].reshape(NB, count, HEADS, HDIM)
    global_keys = jnp.broadcast_to(key_rows[positions].reshape(1, NGLOB, HEADS, HDIM), (NB, NGLOB, HEADS, HDIM))
    global_values = jnp.broadcast_to(value_rows[positions].reshape(1, NGLOB, HEADS, HDIM), (NB, NGLOB, HEADS, HDIM))
    all_keys = jnp.concatenate([picked_keys, global_keys], axis=1).astype(jnp.float32)
    all_values = jnp.concatenate([picked_values, global_values], axis=1).astype(jnp.float32)
    query_blocks = queries.reshape(NB, BLOCK, HEADS, HDIM).astype(jnp.float32)
    scores = jnp.einsum('bqhd,bkhd->bhqk', query_blocks, all_keys) * scale
    top_score = lax.optimization_barrier(jnp.max(scores, axis=-1, keepdims=True))
    expo = jnp.exp(scores - top_score)
    probs = (expo / lax.optimization_barrier(jnp.sum(expo, axis=-1, keepdims=True))).astype(jnp.bfloat16)
    sparse_out = jnp.einsum('bhqk,bkhd->bqhd', probs.astype(jnp.float32), all_values)
    sparse_out = sparse_out.reshape(TOKENS, D).astype(jnp.bfloat16)
    global_queries = queries[positions].astype(jnp.float32).reshape(NGLOB, HEADS, HDIM)
    full_keys = key_rows.astype(jnp.float32).reshape(TOKENS, HEADS, HDIM)
    full_values = value_rows.astype(jnp.float32).reshape(TOKENS, HEADS, HDIM)
    global_scores = jnp.einsum('qhd,khd->hqk', global_queries, full_keys) * scale
    global_top = lax.optimization_barrier(jnp.max(global_scores, axis=-1, keepdims=True))
    global_expo = jnp.exp(global_scores - global_top)
    global_probs = global_expo / lax.optimization_barrier(jnp.sum(global_expo, axis=-1, keepdims=True))
    global_out = jnp.einsum('hqk,khd->qhd', global_probs, full_values, precision=lax.Precision.HIGHEST)
    global_out = global_out.reshape(NGLOB, D).astype(jnp.bfloat16)
    mixed = sparse_out.at[positions].set(global_out)
    return jnp.dot(mixed, out_weight, preferred_element_type=jnp.float32).astype(jnp.bfloat16)
```

```python
import functools
import math

import jax
import jax.numpy as jnp
from jax import lax
from jax.experimental import pallas as pl
from jax.experimental.pallas import tpu as pltpu
from jax.sharding import PartitionSpec as P

HEADS = 16
HDIM = 64
BLOCK = 64
RAND = 3
NGLOB = 128
GROUP = 4
GW = GROUP * HDIM
TILE = 32
EXP2 = HDIM ** (-0.5) * math.log2(math.e)
F32 = jnp.float32
BF16 = jnp.bfloat16
ANY = pl.BlockSpec(memory_space=pl.ANY)
VMEM = pl.BlockSpec(memory_space=pltpu.VMEM)
SMEM = pl.BlockSpec(memory_space=pltpu.SMEM)


def params(mib):
    return pltpu.CompilerParams(vmem_limit_bytes=mib << 20)


def exchange(value, shift):
    count = lax.axis_size("seq")
    return lax.ppermute(value, "seq", [(i, i ^ shift) for i in range(count)])


def layer_norm(tokens, gain):
    values = tokens.astype(F32)
    center = values - jnp.mean(values, axis=-1, keepdims=True)
    spread = jnp.mean(center * center, axis=-1, keepdims=True)
    return (center * lax.rsqrt(spread + 1e-05) * gain).astype(BF16)


def project_kernel(pieces, weights, *refs):
    token_refs = refs[:pieces]
    gain_ref = refs[pieces]
    weight_refs = refs[pieces + 1 : pieces + 1 + weights]
    outs = refs[pieces + 1 + weights : -5]
    weight_buf, normed, result, in_sem, out_sem = refs[-5:]
    rows, width = normed.shape
    loads = []
    for index, weight in enumerate(weight_refs):
        load = pltpu.make_async_copy(weight, weight_buf.at[index], in_sem.at[index])
        load.start()
        loads.append(load)
    at = 0
    for piece in token_refs:
        step = 128
        for start in range(0, piece.shape[0], step):
            normed[at : at + step, :] = layer_norm(piece[start : start + step, :], gain_ref[...])
            at += step
    stores = []
    for index in range(weights):
        loads[index].wait()
        for column in range(0, width, 256):
            result[index, :, column : column + 256] = jnp.dot(
                normed[...],
                weight_buf[index, :, column : column + 256],
                preferred_element_type=F32,
            ).astype(BF16)
        if index < 2:
            target = outs[0].at[:, index * width : (index + 1) * width]
        else:
            target = outs[1]
        store = pltpu.make_async_copy(result.at[index], target, out_sem.at[index])
        store.start()
        stores.append(store)
    for store in stores:
        store.wait()


def project(pieces, gain, weights):
    rows = sum(piece.shape[0] for piece in pieces)
    width = gain.shape[1]
    count = len(weights)
    shapes = [jax.ShapeDtypeStruct((rows, 2 * width), BF16)]
    if count > 2:
        shapes.append(jax.ShapeDtypeStruct((rows, width), BF16))
    return pl.pallas_call(
        functools.partial(project_kernel, len(pieces), count),
        out_shape=shapes,
        in_specs=[VMEM] * (len(pieces) + 1) + [ANY] * count,
        out_specs=[ANY] * len(shapes),
        scratch_shapes=[
            pltpu.VMEM((count, width, width), BF16),
            pltpu.VMEM((rows, width), BF16),
            pltpu.VMEM((count, rows, width), BF16),
            pltpu.SemaphoreType.DMA((count,)),
            pltpu.SemaphoreType.DMA((count,)),
        ],
        compiler_params=params(24),
        cost_estimate=pl.CostEstimate(
            flops=2 * rows * width * width * count,
            bytes_accessed=2 * width * (width * count + rows * (count + 1)),
            transcendentals=rows,
        ),
        name="project",
    )(*pieces, gain, *weights)


def head_masks(rows, dtype):
    lane = lax.broadcasted_iota(jnp.int32, (rows, GW), 1) // HDIM
    return [(lane == head).astype(dtype) for head in range(GROUP)]


def spread_heads(rows):
    masks = head_masks(rows.shape[0], BF16)
    return jnp.concatenate([rows * mask for mask in masks], axis=0)


def pick_heads(stacked, rows):
    lane = lax.broadcasted_iota(jnp.int32, (rows, GW), 1) // HDIM
    picked = stacked[(GROUP - 1) * rows :]
    for head in range(GROUP - 1):
        picked = jnp.where(lane == head, stacked[head * rows : (head + 1) * rows], picked)
    return picked


def contract_last(left, right):
    return lax.dot_general(
        left, right, (((1,), (1,)), ((), ())), preferred_element_type=F32
    )


def token_positions(devs, index, rows):
    lane = lax.broadcasted_iota(jnp.int32, (1, rows), 1)
    owner = jnp.where(lane < rows // 2, devs[2 * index], devs[2 * index + 1])
    return owner * rows + lane


def gather_global(pos, devs, base, kv_refs, columns):
    total = None
    for index, kv in enumerate(kv_refs):
        select = (pos == token_positions(devs, base + index, kv.shape[0])).astype(BF16)
        part = jnp.dot(select, kv[:, columns], preferred_element_type=F32)
        total = part if total is None else total + part
    return total


def global_partial(count, gq, kv_refs, scores, top_ref, sum_ref, acc_ref):
    width = gq.shape[1]

    def one_tile(tile, carry):
        rows = pl.ds(pl.multiple_of(tile * TILE, TILE), TILE)
        for group in range(width // GW):
            columns = slice(group * GW, (group + 1) * GW)
            values = slice(width + group * GW, width + (group + 1) * GW)
            left = spread_heads(gq[rows, columns])
            at = 0
            for kv in kv_refs:
                keys = kv.shape[0]
                scores[:, at : at + keys] = contract_last(left, kv[:, columns])
                at += keys
            top = jnp.max(scores[...], axis=1, keepdims=True)
            total = jnp.zeros_like(top)
            acc = jnp.zeros((GROUP * TILE, GW), F32)
            at = 0
            for kv in kv_refs:
                keys = kv.shape[0]
                probs = jnp.exp2((scores[:, at : at + keys] - top) * EXP2)
                total += jnp.sum(probs, axis=1, keepdims=True)
                acc += jnp.dot(probs.astype(BF16), kv[:, values], preferred_element_type=F32)
                at += keys
            shape = (GROUP * TILE, GW)
            top_ref[rows, columns] = pick_heads(jnp.broadcast_to(top, shape), TILE)
            sum_ref[rows, columns] = pick_heads(jnp.broadcast_to(total, shape), TILE)
            acc_ref[rows, columns] = pick_heads(acc, TILE)
        return carry

    lax.fori_loop(0, (count + TILE - 1) // TILE, one_tile, 0)


def early_kernel(arrays, *refs):
    devs, count, pos, local, queries = refs[:5]
    kv_refs = refs[5 : 5 + arrays]
    gq, gkv, top, total, acc, scores = refs[5 + arrays :]
    rows, width = queries.shape
    lane = lax.broadcasted_iota(jnp.int32, (1, rows), 1)
    select = (local[...] == lane).astype(BF16)
    for column in range(0, width, 256):
        columns = slice(column, column + 256)
        gq[:, columns] = jnp.dot(
            select, queries[:, columns], preferred_element_type=F32
        ).astype(BF16)
    for column in range(0, 2 * width, 256):
        columns = slice(column, column + 256)
        gkv[:, columns] = gather_global(pos[...], devs, 0, kv_refs, columns).astype(BF16)
    global_partial(count[0], gq, kv_refs, scores, top, total, acc)


def early(devs, count, pos, local, queries, kv):
    rows, width = queries.shape
    keys = rows * len(kv)
    state = jax.ShapeDtypeStruct((NGLOB, width), F32)
    return pl.pallas_call(
        functools.partial(early_kernel, len(kv)),
        out_shape=[
            jax.ShapeDtypeStruct((NGLOB, width), BF16),
            jax.ShapeDtypeStruct((NGLOB, 2 * width), BF16),
            state,
            state,
            state,
        ],
        in_specs=[SMEM, SMEM] + [VMEM] * (3 + len(kv)),
        out_specs=[VMEM] * 5,
        scratch_shapes=[pltpu.VMEM((GROUP * TILE, keys), F32)],
        compiler_params=params(56),
        cost_estimate=pl.CostEstimate(
            flops=8 * TILE * keys * width * 2,
            bytes_accessed=4 * width * keys,
            transcendentals=TILE * HEADS * keys,
        ),
        name="early",
    )(devs, count, pos, local, queries, *kv)


def late_kernel(arrays, late, *refs):
    devs, count, ids, offsets, pos, local_row, queries, gq, gkv = refs[:9]
    top1, sum1, acc1, out_weight = refs[9:13]
    kv_refs = refs[13 : 13 + arrays]
    out = refs[13 + arrays]
    keys, weight, last, mixed, top2, sum2, acc2, placed, scores, sems, sem2 = refs[14 + arrays :]
    rows, width = queries.shape
    blocks = rows // BLOCK
    picks = 3 + RAND
    span = picks * BLOCK

    def copies(block, slot, act):
        for pick in range(picks):
            entry = block * picks + pick
            source = ids[entry]
            start = pl.multiple_of(offsets[entry], BLOCK)
            target = keys.at[slot, pl.ds(pick * BLOCK, BLOCK), :]
            if act == "wait":
                pltpu.make_async_copy(
                    kv_refs[0].at[pl.ds(0, BLOCK), :], target, sems.at[slot, pick]
                ).wait()
                continue
            for index in range(arrays):

                @pl.when(source == index)
                def _():
                    pltpu.make_async_copy(
                        kv_refs[index].at[pl.ds(start, BLOCK), :], target, sems.at[slot, pick]
                    ).start()

    loads = [
        pltpu.make_async_copy(kv_refs[arrays - late + i], last.at[i], sem2.at[i])
        for i in range(late)
    ]
    for load in loads:
        load.start()
    copies(0, 0, "start")
    weight_load = pltpu.make_async_copy(out_weight, weight, sem2.at[late])
    weight_load.start()
    for load in loads:
        load.wait()
    final_refs = [last.at[i] for i in range(late)]
    for column in range(0, 2 * width, 256):
        columns = slice(column, column + 256)
        gathered = gkv[:, columns] + gather_global(
            pos[...], devs, arrays - late, final_refs, columns
        ).astype(BF16)
        keys[0, span:, columns] = gathered
        keys[1, span:, columns] = gathered
    placed[...] = jnp.zeros_like(placed)
    global_partial(count[0], gq, final_refs, scores, top2, sum2, acc2)

    def merge(tile, carry):
        at = pl.ds(pl.multiple_of(tile * TILE, TILE), TILE)
        top = jnp.maximum(top1[at, :], top2[at, :])
        one = jnp.exp2((top1[at, :] - top) * EXP2)
        two = jnp.exp2((top2[at, :] - top) * EXP2)
        total = sum1[at, :] * one + sum2[at, :] * two
        placed[at, :] = ((acc1[at, :] * one + acc2[at, :] * two) / total).astype(BF16)
        return carry

    lax.fori_loop(0, (count[0] + TILE - 1) // TILE, merge, 0)

    def one_block(block, carry):
        slot = lax.rem(block, 2)

        @pl.when(block + 1 < blocks)
        def _():
            copies(block + 1, 1 - slot, "start")

        copies(block, slot, "wait")
        at = pl.ds(pl.multiple_of(block * BLOCK, BLOCK), BLOCK)
        for group in range(width // GW):
            columns = slice(group * GW, (group + 1) * GW)
            values = slice(width + group * GW, width + (group + 1) * GW)
            left = spread_heads(queries[at, columns])
            score = contract_last(left, keys[slot, :, columns])
            top = jnp.max(score, axis=1, keepdims=True)
            probs = jnp.exp2((score - top) * EXP2)
            total = jnp.sum(probs, axis=1, keepdims=True)
            weighted = jnp.dot(
                probs.astype(BF16), keys[slot, :, values], preferred_element_type=F32
            )
            mixed[at, columns] = pick_heads(weighted / total, BLOCK).astype(BF16)
        return carry

    lax.fori_loop(0, blocks, one_block, 0)
    row = lax.broadcasted_iota(jnp.int32, (rows, NGLOB), 0)
    select = row == local_row[...]
    owned = jnp.max(select.astype(F32), axis=1, keepdims=True) > 0.5
    select = select.astype(BF16)
    for column in range(0, width, 256):
        columns = slice(column, column + 256)
        moved = jnp.dot(select, placed[:, columns], preferred_element_type=F32).astype(BF16)
        mixed[:, columns] = jnp.where(owned, moved, mixed[:, columns])
    weight_load.wait()
    for column in range(0, width, 256):
        columns = slice(column, column + 256)
        out[:, columns] = jnp.dot(
            mixed[...], weight[:, columns], preferred_element_type=F32
        ).astype(BF16)


def finish(late, devs, count, ids, offsets, pos, local_row, queries, state, out_weight, kv):
    rows, width = queries.shape
    keys = (3 + RAND) * BLOCK + NGLOB
    return pl.pallas_call(
        functools.partial(late_kernel, len(kv), late),
        out_shape=jax.ShapeDtypeStruct((rows, width), BF16),
        in_specs=[SMEM] * 4 + [VMEM] * 8 + [ANY] * (1 + len(kv)),
        out_specs=VMEM,
        scratch_shapes=[
            pltpu.VMEM((2, keys, 2 * width), BF16),
            pltpu.VMEM((width, width), BF16),
            pltpu.VMEM((late, rows, 2 * width), BF16),
            pltpu.VMEM((rows, width), BF16),
            pltpu.VMEM((NGLOB, width), F32),
            pltpu.VMEM((NGLOB, width), F32),
            pltpu.VMEM((NGLOB, width), F32),
            pltpu.VMEM((NGLOB, width), BF16),
            pltpu.VMEM((GROUP * TILE, late * rows), F32),
            pltpu.SemaphoreType.DMA((2, 3 + RAND)),
            pltpu.SemaphoreType.DMA((late + 1,)),
        ],
        compiler_params=params(48),
        name="finish",
    )(devs, count, ids, offsets, pos, local_row, queries, *state, out_weight, *kv)


def body(
    tokens,
    norm_gain,
    query_weight,
    key_weight,
    value_weight,
    out_weight,
    random_blocks,
    bucket_id,
    global_positions,
):
    shards = lax.axis_size("seq")
    device = lax.axis_index("seq").astype(jnp.int32)
    rows = tokens.shape[0]
    width = tokens.shape[1]
    local_blocks = rows // BLOCK
    half = rows // 2
    gain = norm_gain.reshape(1, width)
    pair = (key_weight, value_weight)

    kv = []
    owners = []
    if shards == 8:
        low, high = tokens[:half], tokens[half:]
        low2, high4 = exchange(low, 2), exchange(high, 4)
        high2, low4 = exchange(high, 2), exchange(low, 4)
        low6, high6 = exchange(low2, 4), exchange(high4, 2)
        own, queries = project([tokens], gain, (*pair, query_weight))
        rounds = [
            (own, 0, 0),
            (project([low2, high4], gain, pair)[0], 2, 4),
            (project([low4, high2], gain, pair)[0], 4, 2),
            (project([low6, high6], gain, pair)[0], 6, 6),
        ]
    else:
        have = {0: tokens}
        bit = 2
        while bit < shards:
            for j in list(have):
                have[j | bit] = exchange(have[j], bit)
            bit *= 2
        own, queries = project([tokens], gain, (*pair, query_weight))
        rounds = [(own, 0, 0)]
        for j in sorted(have)[1:]:
            rounds.append((project([have[j]], gain, pair)[0], j, j))
    for array, first, second in rounds:
        kv += [array, exchange(array, 1)]
        owners += [first, second, first ^ 1, second ^ 1]
    devs = device ^ jnp.array(owners, jnp.int32)

    block = device * local_blocks + jnp.arange(local_blocks, dtype=jnp.int32)
    total = shards * local_blocks
    window = jnp.stack([(block + total - 1) % total, block, (block + 1) % total], axis=1)
    mine = lax.dynamic_slice_in_dim(random_blocks, device * local_blocks, local_blocks, 0)
    chosen = jnp.concatenate([window, mine.astype(jnp.int32)], axis=1).reshape(-1)
    inner = chosen % local_blocks
    slot = (chosen // local_blocks) ^ device
    if shards == 8:
        upper = (inner >= local_blocks // 2).astype(jnp.int32)
        hop = slot >> 1
        step = jnp.where(hop == 1, 1 + upper, jnp.where(hop == 2, 2 - upper, hop))
        ids = 2 * step + (slot & 1)
    else:
        ids = slot
    offsets = inner * BLOCK

    positions = lax.dynamic_index_in_dim(global_positions, bucket_id[0], 0, False)
    positions = positions.astype(jnp.int32)
    local = positions - device * rows
    first = jnp.sum((local < 0).astype(jnp.int32))
    count = jnp.sum(((local >= 0) & (local < rows)).astype(jnp.int32)).reshape(1)
    padded = jnp.concatenate([local, jnp.full((NGLOB,), -1, jnp.int32)])
    compact = lax.dynamic_slice_in_dim(padded, first, NGLOB, 0)
    pos = positions.reshape(NGLOB, 1)

    state = early(devs, count, pos, compact.reshape(NGLOB, 1), queries, kv[:-2])
    return finish(
        2,
        devs,
        count,
        ids,
        offsets,
        pos,
        compact.reshape(1, NGLOB),
        queries,
        state,
        out_weight,
        kv,
    )


def solution(mesh):
    placed = (P(("dp", "seq"), None), P(), P(), P(), P(), P(), P("dp", None), P(), P())
    return jax.shard_map(
        body, mesh=mesh, in_specs=placed, out_specs=P(("dp", "seq"), None), check_vma=False
    )
```

```python
import functools
import math

import jax
import jax.numpy as jnp
from jax import lax
from jax.experimental import pallas as pl
from jax.experimental.pallas import tpu as pltpu
from jax.sharding import PartitionSpec as P

HEADS = 16
HDIM = 64
BLOCK = 64
RAND = 3
NGLOB = 128
GROUP = 4
GW = GROUP * HDIM
TILE = 32
PICKS = 3 + RAND
EXP2 = HDIM ** (-0.5) * math.log2(math.e)
F32 = jnp.float32
BF16 = jnp.bfloat16
HBM = pl.BlockSpec(memory_space=pltpu.HBM)
VMEM = pl.BlockSpec(memory_space=pltpu.VMEM)
SMEM = pl.BlockSpec(memory_space=pltpu.SMEM)
COST = pl.CostEstimate(flops=1024, bytes_accessed=1024, transcendentals=0)


def params(mib):
    return pltpu.CompilerParams(vmem_limit_bytes=mib << 20)


LIMIT = 60


def hops_of(shards):
    if shards == 8:
        return [(0, 0), (2, 4), (4, 2), (6, 6)]
    return [(2 * step, 2 * step) for step in range(shards // 2)]


def layer_norm(tokens, gain):
    values = tokens.astype(F32)
    center = values - jnp.mean(values, axis=-1, keepdims=True)
    spread = jnp.mean(center * center, axis=-1, keepdims=True)
    return (center * lax.rsqrt(spread + 1e-05) * gain).astype(BF16)


def head_lane(rows):
    return lax.broadcasted_iota(jnp.int32, (rows, GW), 1) // HDIM


def spread_heads(rows):
    lane = head_lane(rows.shape[0])
    masks = [(lane == head).astype(BF16) for head in range(GROUP)]
    return jnp.concatenate([rows * mask for mask in masks], axis=0)


def pick_heads(stacked, rows):
    lane = head_lane(rows)
    picked = stacked[(GROUP - 1) * rows :]
    for head in range(GROUP - 1):
        picked = jnp.where(lane == head, stacked[head * rows : (head + 1) * rows], picked)
    return picked


def contract_last(left, right):
    return lax.dot_general(left, right, (((1,), (1,)), ((), ())), preferred_element_type=F32)


def square(axis):
    return lax.broadcasted_iota(jnp.int32, (NGLOB, NGLOB), axis)


class Globals:
    def __init__(self, bucket, table, rows):
        self.me = lax.axis_index("seq")
        self.rows = rows
        self.row = table[pl.ds(bucket[0], 1), :]
        self.local = self.row - self.me * rows
        self.first = jnp.sum((self.local < 0).astype(F32)).astype(jnp.int32)
        below = jnp.sum((self.local < rows).astype(F32)).astype(jnp.int32)
        self.count = below - self.first
        self.tiles = (self.count + TILE - 1) // TILE

    def column(self):
        spread = jnp.where(square(0) == square(1), self.row, 0).astype(F32)
        return jnp.sum(spread, axis=1, keepdims=True).astype(jnp.int32)

    def own_column(self):
        hit = jnp.where(square(1) == square(0) + self.first, self.local, 0).astype(F32)
        found = jnp.sum(hit, axis=1, keepdims=True).astype(jnp.int32)
        index = lax.broadcasted_iota(jnp.int32, (NGLOB, 1), 0)
        return jnp.where(index < self.count, found, -1)

    def own_row(self):
        local = self.column() - self.me * self.rows
        hit = jnp.where(square(0) == square(1) + self.first, local, 0).astype(F32)
        found = jnp.sum(hit, axis=0, keepdims=True).astype(jnp.int32)
        index = lax.broadcasted_iota(jnp.int32, (1, NGLOB), 1)
        return jnp.where(index < self.count, found, -1)


def owner(me, step, core, shards):
    even, odd = hops_of(shards)[step]
    there = me ^ core
    return there ^ jnp.where(there & 1 == 0, even, odd)


def place_of(device, me, shards):
    slot = device ^ me
    core = slot & 1
    hop = slot - core
    if shards != 8:
        return hop // 2, core
    parity = (me ^ core) & 1
    near = jnp.where((hop == 2) == (parity == 0), 1, 2)
    return jnp.where(hop == 0, 0, jnp.where(hop == 6, 3, near)), core


def start_loads(sources, targets, sems):
    loads = []
    for index, (source, target) in enumerate(zip(sources, targets)):
        load = pltpu.make_async_copy(source, target, sems.at[index])
        load.start()
        loads.append(load)
    return loads


def normalize(loads, tokens, gain, normed, info, bases):
    pieces, rows, width = tokens.shape
    total = pieces * rows
    for piece in range(pieces):
        loads[piece].wait()
        for start in range(0, rows, 128):
            at = piece * rows + start
            normed[at : at + 128, :] = layer_norm(tokens[piece, start : start + 128, :], gain[...])
    lane = lax.broadcasted_iota(jnp.int32, (1, total), 1)
    column = info.column()
    where = jnp.full((NGLOB, 1), -1, jnp.int32)
    for piece, base in enumerate(bases):
        inside = column - base * rows
        hit = jnp.where(inside < 0, rows, inside) < rows
        where = jnp.where(hit, inside + piece * rows, where)
    select = (where == lane).astype(BF16)
    for start in range(0, width, 256):
        columns = slice(start, start + 256)
        normed[total:, columns] = jnp.dot(
            select, normed[:total, columns], preferred_element_type=F32
        ).astype(BF16)


def multiply(normed, weight, results, offset):
    for start in range(0, weight.shape[1], 256):
        results[:, offset + start : offset + start + 256] = jnp.dot(
            normed[...], weight[:, start : start + 256], preferred_element_type=F32
        ).astype(BF16)


def global_partial(tiles, gq, kv, total, scores, state):
    width = gq.shape[1]

    def one_tile(tile, carry):
        at = pl.ds(pl.multiple_of(tile * TILE, TILE), TILE)
        for group in range(width // GW):
            columns = slice(group * GW, (group + 1) * GW)
            values = slice(width + group * GW, width + (group + 1) * GW)
            left = spread_heads(gq[at, columns])
            scores[...] = contract_last(left, kv[:total, columns])
            top = jnp.max(scores[...], axis=1, keepdims=True)
            probs = jnp.exp2((scores[...] - top) * EXP2)
            part = jnp.sum(probs, axis=1, keepdims=True)
            acc = jnp.dot(probs.astype(BF16), kv[:total, values], preferred_element_type=F32)
            shape = (GROUP * TILE, GW)
            for index, value in enumerate(
                (jnp.broadcast_to(top, shape), jnp.broadcast_to(part, shape), acc)
            ):
                state[index, at, columns] = pick_heads(value, TILE)
        return carry

    lax.fori_loop(0, tiles, one_tile, 0)


def move_state(tiles, pairs, sems, act):
    for tile in range(NGLOB // TILE):

        @pl.when(tile < tiles)
        def _():
            rows = slice(tile * TILE, (tile + 1) * TILE)
            for index, (source, target) in enumerate(pairs):
                copy = pltpu.make_async_copy(
                    source.at[:, rows, :], target.at[:, rows, :], sems.at[tile, index]
                )
                copy.start() if act == "start" else copy.wait()


def merge_states(tiles, states, target):
    def one_tile(tile, carry):
        at = pl.ds(pl.multiple_of(tile * TILE, TILE), TILE)
        top = functools.reduce(jnp.maximum, [ref[0, at, :] for ref in states])
        total = jnp.zeros_like(top)
        acc = jnp.zeros_like(top)
        for ref in states:
            factor = jnp.exp2((ref[0, at, :] - top) * EXP2)
            total += ref[1, at, :] * factor
            acc += ref[2, at, :] * factor
        target[at, :] = (acc / total).astype(BF16)
        return carry

    lax.fori_loop(0, tiles, one_tile, 0)


def rows_kernel(shards, places, *refs):
    count = len(places)
    first = places[0][0] == 0
    bucket, table, gain = refs[:3]
    sources = refs[3 : 3 + count]
    weights = refs[3 + count : 5 + count + first]
    at = 5 + count + first
    if first:
        out, gsum, kept, queries, gq = refs[at : at + 5]
        at += 5
    else:
        gq, gold, out, gsum, kept = refs[at : at + 5]
        at += 5
    tokens, weight, normed, results, state, scores, token_sems, weight_sems, out_sems, sems = refs[
        at : at + 10
    ]
    rows, width = sources[0].shape
    total = count * rows
    loads = start_loads(sources, [tokens.at[i] for i in range(count)], token_sems)
    order = [2, 0, 1] if first else [0, 1]
    arrivals = start_loads(
        [weights[i] for i in order], [weight.at[i] for i in order], weight_sems
    )
    info = Globals(bucket, table, rows)
    bases = [owner(info.me, step, core, shards) for step, core in places]
    normalize(loads, tokens, gain, normed, info, bases)
    if first:
        arrivals.pop(0).wait()
        lane = lax.broadcasted_iota(jnp.int32, (1, rows), 1)
        select = (info.own_column() == lane).astype(BF16)
        for start in range(0, width, 256):
            columns = slice(start, start + 256)
            query = jnp.dot(
                normed[:rows, :], weight[2, :, columns], preferred_element_type=F32
            ).astype(BF16)
            queries[:, columns] = query
            gq[:, columns] = jnp.dot(select, query, preferred_element_type=F32).astype(BF16)
    stores = []
    for index in range(2):
        arrivals[index].wait()
        multiply(normed, weight.at[index], results, index * width)
        columns = slice(index * width, (index + 1) * width)
        store = pltpu.make_async_copy(
            results.at[:total, columns], out.at[:, columns], out_sems.at[index]
        )
        store.start()
        stores.append(store)
    gsum[...] = results[total:, :] if first else gold[...] + results[total:, :]
    global_partial(info.tiles, gq, results, total, scores, state)
    move_state(info.tiles, [(state, kept)], sems, "start")
    move_state(info.tiles, [(state, kept)], sems, "wait")
    for store in stores:
        store.wait()


def call(kernel, inputs, specs, outs, out_specs, scratch, name):
    return pl.pallas_call(
        kernel,
        out_shape=[jax.ShapeDtypeStruct(*out) for out in outs],
        in_specs=specs,
        out_specs=out_specs,
        scratch_shapes=scratch,
        compiler_params=params(LIMIT),
        cost_estimate=COST,
        name=name,
    )(*inputs)


def project_scratch(count, rows, width, weights):
    total = count * rows + NGLOB
    return [
        pltpu.VMEM((count, rows, width), BF16),
        pltpu.VMEM((weights, width, width), BF16),
        pltpu.VMEM((total, width), BF16),
        pltpu.VMEM((total, 2 * width), BF16),
        pltpu.VMEM((3, NGLOB, width), F32),
        pltpu.VMEM((GROUP * TILE, count * rows), F32),
        pltpu.SemaphoreType.DMA((count,)),
        pltpu.SemaphoreType.DMA((weights,)),
    ]


def rows_call(shards, places, index, gain, pieces, weights, *chain):
    rows, width = pieces[0].shape
    first = places[0][0] == 0
    outs = [
        ((len(pieces) * rows, 2 * width), BF16),
        ((NGLOB, 2 * width), BF16),
        ((3, NGLOB, width), F32),
    ]
    if first:
        outs += [((rows, width), BF16), ((NGLOB, width), BF16)]
    return call(
        functools.partial(rows_kernel, shards, places),
        [*index, gain, *pieces, *weights, *chain],
        [SMEM, VMEM, VMEM] + [HBM] * (len(pieces) + len(weights)) + [VMEM] * len(chain),
        outs,
        [HBM, VMEM, HBM] + [VMEM] * (2 * first),
        project_scratch(len(pieces), rows, width, len(weights))
        + [pltpu.SemaphoreType.DMA((2,)), pltpu.SemaphoreType.DMA((NGLOB // TILE, 1))],
        "first" if first else "middle",
    )


def last_kernel(shards, parts, places, *refs):
    bucket, table, blocks_ref, gain, gq, gold, queries = refs[:7]
    sources = refs[7:9]
    weights = refs[9:12]
    part_refs = refs[12 : 12 + parts]
    kv_refs = refs[12 + parts : 12 + 2 * parts]
    out = refs[12 + 2 * parts]
    tokens, weight, normed, results, state, scores, token_sems, weight_sems = refs[
        13 + 2 * parts : 21 + 2 * parts
    ]
    keys, mixed, placed, olds, sems, state_sems = refs[21 + 2 * parts :]
    rows, width = queries.shape
    total = 2 * rows
    blocks = rows // BLOCK
    span = PICKS * BLOCK
    total_blocks = shards * blocks
    steps = shards // 2
    loads = start_loads(sources, [tokens.at[i] for i in range(2)], token_sems)
    arrivals = start_loads(weights, [weight.at[i] for i in range(3)], weight_sems)
    info = Globals(bucket, table, rows)
    me = info.me
    olds_refs = [olds.at[i] for i in range(parts)]
    pairs = list(zip(part_refs, olds_refs))
    move_state(info.tiles, pairs, state_sems, "start")

    def copies(block, slot, act):
        for pick in range(PICKS):
            target = keys.at[slot, pl.ds(pick * BLOCK, BLOCK), :]
            sem = sems.at[slot, pick]
            if act == "wait":
                pltpu.make_async_copy(kv_refs[0].at[pl.ds(0, BLOCK), :], target, sem).wait()
                continue
            here = me * blocks + block
            if pick < 3:
                chosen = lax.rem(here + total_blocks + pick - 1, total_blocks)
            else:
                chosen = blocks_ref[here, pick - 3]
            device = chosen // blocks
            step, core = place_of(device, me, shards)
            flat = jnp.where(step == 0, core, 2 * step - 2 + core)
            late = step == steps - 1
            piece = jnp.where(late, core, flat % 4)
            source = jnp.where(step == 0, 0, jnp.where(late, parts, 1 + flat // 4))
            start = piece * rows + (chosen - device * blocks) * BLOCK
            start = pl.multiple_of(start, BLOCK)
            for index in range(parts + 1):
                held = results if index == parts else kv_refs[index]

                @pl.when(source == index)
                def _():
                    pltpu.make_async_copy(held.at[pl.ds(start, BLOCK), :], target, sem).start()

    bases = [owner(me, step, core, shards) for step, core in places]
    normalize(loads, tokens, gain, normed, info, bases)
    for index in range(2):
        arrivals[index].wait()
        multiply(normed, weight.at[index], results, index * width)
    copies(0, 0, "start")
    gathered = gold[...] + results[total:, :]
    keys[0, span:, :] = gathered
    keys[1, span:, :] = gathered
    placed[...] = jnp.zeros_like(placed)
    global_partial(info.tiles, gq, results, total, scores, state)
    move_state(info.tiles, pairs, state_sems, "wait")
    merge_states(info.tiles, [state, *olds_refs], placed)

    def one_block(block, carry):
        slot = lax.rem(block, 2)

        @pl.when(block + 1 < blocks)
        def _():
            copies(block + 1, 1 - slot, "start")

        copies(block, slot, "wait")
        at = pl.ds(pl.multiple_of(block * BLOCK, BLOCK), BLOCK)
        groups = range(width // GW)
        score = [
            contract_last(
                spread_heads(queries[at, g * GW : (g + 1) * GW]),
                keys[slot, :, g * GW : (g + 1) * GW],
            )
            for g in groups
        ]
        probs = []
        totals = []
        for g in groups:
            top = jnp.max(score[g], axis=1, keepdims=True)
            prob = jnp.exp2((score[g] - top) * EXP2)
            totals.append(jnp.sum(prob, axis=1, keepdims=True))
            probs.append(prob.astype(BF16))
        for g in groups:
            weighted = jnp.dot(
                probs[g],
                keys[slot, :, width + g * GW : width + (g + 1) * GW],
                preferred_element_type=F32,
            )
            mixed[at, g * GW : (g + 1) * GW] = pick_heads(
                weighted * (1.0 / totals[g]), BLOCK
            ).astype(BF16)
        return carry

    lax.fori_loop(0, blocks, one_block, 0)
    row = lax.broadcasted_iota(jnp.int32, (rows, NGLOB), 0)
    select = row == info.own_row()
    owned = jnp.max(select.astype(F32), axis=1, keepdims=True) > 0.5
    select = select.astype(BF16)
    for column in range(0, width, 256):
        columns = slice(column, column + 256)
        moved = jnp.dot(select, placed[:, columns], preferred_element_type=F32).astype(BF16)
        mixed[:, columns] = jnp.where(owned, moved, mixed[:, columns])
    arrivals[2].wait()
    for column in range(0, width, 256):
        columns = slice(column, column + 256)
        out[:, columns] = jnp.dot(
            mixed[...], weight[2, :, columns], preferred_element_type=F32
        ).astype(BF16)


def last_call(shards, places, index, random_blocks, gain, gq, gold, queries, pieces, weights, parts, kv):
    rows, width = queries.shape
    keys = PICKS * BLOCK + NGLOB
    return call(
        functools.partial(last_kernel, shards, len(parts), places),
        [*index, random_blocks, gain, gq, gold, queries, *pieces, *weights, *parts, *kv],
        [SMEM, VMEM, SMEM] + [VMEM] * 4 + [HBM] * (5 + 2 * len(parts)),
        [((rows, width), BF16)],
        [VMEM],
        project_scratch(2, rows, width, 3)
        + [
            pltpu.VMEM((2, keys, 2 * width), BF16),
            pltpu.VMEM((rows, width), BF16),
            pltpu.VMEM((NGLOB, width), BF16),
            pltpu.VMEM((len(parts), 3, NGLOB, width), F32),
            pltpu.SemaphoreType.DMA((2, PICKS)),
            pltpu.SemaphoreType.DMA((NGLOB // TILE, len(parts))),
        ],
        "last",
    )[0]


def exchange(value, even, odd):
    count = lax.axis_size("seq")
    return lax.ppermute(value, "seq", [(i, i ^ (odd if i & 1 else even)) for i in range(count)])


def body(
    tokens,
    norm_gain,
    query_weight,
    key_weight,
    value_weight,
    out_weight,
    random_blocks,
    bucket_id,
    global_positions,
):
    shards = lax.axis_size("seq")
    width = tokens.shape[1]
    gain = norm_gain.reshape(1, width)
    pair = [key_weight, value_weight]
    index = [bucket_id, global_positions]
    steps = shards // 2
    if shards == 8:
        arrived = [tokens, exchange(tokens, 2, 4), exchange(tokens, 4, 2), None]
    else:
        arrived = [tokens] + [None] * (steps - 1)
        bit = 1
        while bit < steps:
            for step in range(bit):
                arrived[step | bit] = exchange(arrived[step], 2 * bit, 2 * bit)
            bit *= 2
    across = [exchange(tokens, 1, 1)]
    kv0, gsum, part, queries, gq = rows_call(
        shards, [(0, 0), (0, 1)], index, gain, [tokens, across[0]], [*pair, query_weight]
    )
    kv = [kv0]
    parts = [part]
    held, *arrived[1:3] = lax.optimization_barrier((gsum, *arrived[1:3]))
    if shards == 8:
        arrived[3] = exchange(arrived[1], 4, 2)
    pieces = []
    for step in range(1, steps - 1):
        pieces += [((step, 0), arrived[step]), ((step, 1), exchange(arrived[step], 1, 1))]
    for at in range(0, len(pieces), 4):
        some = pieces[at : at + 4]
        now, held, part = rows_call(
            shards, [p for p, _ in some], index, gain, [v for _, v in some], pair, gq, held
        )
        kv.append(now)
        parts.append(part)
    fresh, held = lax.optimization_barrier((arrived[-1], held))
    return last_call(
        shards,
        [(steps - 1, 0), (steps - 1, 1)],
        index,
        random_blocks,
        gain,
        gq,
        held,
        queries,
        [fresh, exchange(fresh, 1, 1)],
        [*pair, out_weight],
        parts,
        kv,
    )


def solution(mesh):
    placed = (P(("dp", "seq"), None), P(), P(), P(), P(), P(), P("dp", None), P(), P())
    return jax.shard_map(
        body, mesh=mesh, in_specs=placed, out_specs=P(("dp", "seq"), None), check_vma=False
    )
```

```python
import functools
import math

import jax
import jax.numpy as jnp
from jax import lax
from jax.experimental import pallas as pl
from jax.experimental.pallas import tpu as pltpu
from jax.sharding import PartitionSpec as P

HEADS = 16
HDIM = 64
BLOCK = 64
RAND = 3
NGLOB = 128
GROUP = 4
GW = GROUP * HDIM
TILE = 32
CHUNK = 256
PICKS = 3 + RAND
EXP2 = HDIM ** (-0.5) * math.log2(math.e)
F32 = jnp.float32
BF16 = jnp.bfloat16
HBM = pl.BlockSpec(memory_space=pltpu.HBM)
VMEM = pl.BlockSpec(memory_space=pltpu.VMEM)
SMEM = pl.BlockSpec(memory_space=pltpu.SMEM)
LATE_COST = pl.CostEstimate(flops=10**11, bytes_accessed=1024, transcendentals=0)
COST = pl.CostEstimate(flops=1024, bytes_accessed=1024, transcendentals=0)


def params(mib):
    return pltpu.CompilerParams(vmem_limit_bytes=mib << 20)


LIMIT = 60


def hops_of(shards):
    if shards == 8:
        return [(0, 0), (2, 4), (4, 2), (6, 6)]
    return [(2 * step, 2 * step) for step in range(shards // 2)]


def layer_norm(tokens, gain):
    values = tokens.astype(F32)
    center = values - jnp.mean(values, axis=-1, keepdims=True)
    spread = jnp.mean(center * center, axis=-1, keepdims=True)
    return (center * lax.rsqrt(spread + 1e-05) * gain).astype(BF16)


def head_lane(rows):
    return lax.broadcasted_iota(jnp.int32, (rows, GW), 1) // HDIM


def spread_heads(rows):
    lane = head_lane(rows.shape[0])
    masks = [(lane == head).astype(BF16) for head in range(GROUP)]
    return jnp.concatenate([rows * mask for mask in masks], axis=0)


def pick_heads(stacked, rows):
    lane = head_lane(rows)
    picked = stacked[(GROUP - 1) * rows :]
    for head in range(GROUP - 1):
        picked = jnp.where(lane == head, stacked[head * rows : (head + 1) * rows], picked)
    return picked


def contract_last(left, right):
    return lax.dot_general(left, right, (((1,), (1,)), ((), ())), preferred_element_type=F32)


def square(axis):
    return lax.broadcasted_iota(jnp.int32, (NGLOB, NGLOB), axis)


class Globals:
    def __init__(self, bucket, table, rows, core=0):
        self.me = lax.axis_index("seq") ^ core
        self.rows = rows
        self.row = table[pl.ds(bucket[0], 1), :]
        self.local = self.row - self.me * rows
        self.first = jnp.sum((self.local < 0).astype(F32)).astype(jnp.int32)
        below = jnp.sum((self.local < rows).astype(F32)).astype(jnp.int32)
        self.count = below - self.first
        self.tiles = (self.count + TILE - 1) // TILE

    def column(self):
        spread = jnp.where(square(0) == square(1), self.row, 0).astype(F32)
        return jnp.sum(spread, axis=1, keepdims=True).astype(jnp.int32)

    def own_column(self):
        hit = jnp.where(square(1) == square(0) + self.first, self.local, 0).astype(F32)
        found = jnp.sum(hit, axis=1, keepdims=True).astype(jnp.int32)
        index = lax.broadcasted_iota(jnp.int32, (NGLOB, 1), 0)
        return jnp.where(index < self.count, found, -1)

    def own_row(self):
        local = self.column() - self.me * self.rows
        hit = jnp.where(square(0) == square(1) + self.first, local, 0).astype(F32)
        found = jnp.sum(hit, axis=0, keepdims=True).astype(jnp.int32)
        index = lax.broadcasted_iota(jnp.int32, (1, NGLOB), 1)
        return jnp.where(index < self.count, found, -1)


def owner(me, step, core, shards):
    even, odd = hops_of(shards)[step]
    there = me ^ core
    return there ^ jnp.where(there & 1 == 0, even, odd)


def place_of(device, me, shards):
    slot = device ^ me
    core = slot & 1
    hop = slot - core
    if shards != 8:
        return hop // 2, core
    parity = (me ^ core) & 1
    near = jnp.where((hop == 2) == (parity == 0), 1, 2)
    return jnp.where(hop == 0, 0, jnp.where(hop == 6, 3, near)), core


def start_loads(sources, targets, sems):
    loads = []
    for index, (source, target) in enumerate(zip(sources, targets)):
        load = pltpu.make_async_copy(source, target, sems.at[index])
        load.start()
        loads.append(load)
    return loads


def select_rows(info, bases, rows):
    lane = lax.broadcasted_iota(jnp.int32, (1, len(bases) * rows), 1)
    column = info.column()
    where = jnp.full((NGLOB, 1), -1, jnp.int32)
    for piece, base in enumerate(bases):
        inside = column - base * rows
        hit = jnp.where(inside < 0, rows, inside) < rows
        where = jnp.where(hit, inside + piece * rows, where)
    return (where == lane).astype(BF16)


def norm_chunk(tokens, gain, normed, at):
    rows = tokens.shape[1]
    piece, start = at // rows, at % rows
    for row in range(0, CHUNK, 64):
        normed[at + row : at + row + 64, :] = layer_norm(
            tokens[piece, start + row : start + row + 64, :], gain[...]
        )


def multiply(normed, at, height, weights, results):
    left = normed[at : at + height, :]
    width = normed.shape[1]
    for index, weight in enumerate(weights):
        for start in range(0, width, 256):
            results[at : at + height, index * width + start : index * width + start + 256] = (
                jnp.dot(
                    left, weight[:, start : start + 256], preferred_element_type=F32
                ).astype(BF16)
            )


def global_partial(tiles, queries, kv, total, scores, states):
    width = queries[0].shape[1]
    stacked = GROUP * TILE
    count = len(queries)

    def one_tile(tile, carry):
        at = pl.ds(pl.multiple_of(tile * TILE, TILE), TILE)
        for group in range(width // GW):
            columns = slice(group * GW, (group + 1) * GW)
            values = slice(width + group * GW, width + (group + 1) * GW)
            left = [spread_heads(ref[at, columns]) for ref in queries]
            left = left[0] if count == 1 else jnp.concatenate(left, axis=0)
            scores[...] = contract_last(left, kv[:total, columns])
            top = jnp.max(scores[...], axis=1, keepdims=True)
            probs = jnp.exp2((scores[...] - top) * EXP2)
            part = jnp.sum(probs, axis=1, keepdims=True)
            acc = jnp.dot(probs.astype(BF16), kv[:total, values], preferred_element_type=F32)
            shape = (count * stacked, GW)
            for index, value in enumerate(
                (jnp.broadcast_to(top, shape), jnp.broadcast_to(part, shape), acc)
            ):
                for which, state in enumerate(states):
                    state[index, at, columns] = pick_heads(
                        value[which * stacked : (which + 1) * stacked], TILE
                    )
        return carry

    lax.fori_loop(0, tiles, one_tile, 0)


def move_state(tiles, pairs, sems, act):
    for tile in range(NGLOB // TILE):

        @pl.when(tile < tiles)
        def _():
            rows = slice(tile * TILE, (tile + 1) * TILE)
            for index, (source, target) in enumerate(pairs):
                copy = pltpu.make_async_copy(
                    source.at[:, rows, :], target.at[:, rows, :], sems.at[tile, index]
                )
                copy.start() if act == "start" else copy.wait()


def merge_states(tiles, states, target):
    def one_tile(tile, carry):
        at = pl.ds(pl.multiple_of(tile * TILE, TILE), TILE)
        top = functools.reduce(jnp.maximum, [ref[0, at, :] for ref in states])
        total = jnp.zeros_like(top)
        acc = jnp.zeros_like(top)
        for ref in states:
            factor = jnp.exp2((ref[0, at, :] - top) * EXP2)
            total += ref[1, at, :] * factor
            acc += ref[2, at, :] * factor
        target[at, :] = (acc / total).astype(BF16)
        return carry

    lax.fori_loop(0, tiles, one_tile, 0)


def rows_kernel(shards, places, kind, *refs):
    count = len(places)
    first = kind == "first"
    sets = 2 if kind == "middle" else 1
    refs = list(refs)

    def take(number):
        taken = refs[:number]
        del refs[:number]
        return taken

    bucket, table, gain = take(3)
    sources = take(count)
    weights = take(2 + first)
    gq_sets = take(0 if first else sets)
    out, gsum = take(2)
    kept = take(sets)
    if first:
        (queries,) = take(1)
        gq_sets = take(1)
    tokens, weight, normed, results, token_sems, weight_sems, out_sems, sems, scores = take(9)
    states = take(sets)
    rows, width = sources[0].shape
    total = count * rows
    loads = start_loads(sources, [tokens.at[i] for i in range(count)], token_sems)
    arrivals = start_loads(weights, [weight.at[i] for i in range(len(weights))], weight_sems)
    info = Globals(bucket, table, rows)
    bases = [owner(info.me, step, core, shards) for step, core in places]
    select = select_rows(info, bases, rows)
    loads[0].wait()
    norm_chunk(tokens, gain, normed, 0)
    for load in loads[1:] + arrivals:
        load.wait()
    pair = [weight.at[0], weight.at[1]]
    stores = []
    for at in range(0, total, CHUNK):
        if at + CHUNK < total:
            norm_chunk(tokens, gain, normed, at + CHUNK)
        multiply(normed, at, CHUNK, pair, results)
        store = pltpu.make_async_copy(
            results.at[at : at + CHUNK, :], out.at[at : at + CHUNK, :], out_sems.at[at // CHUNK]
        )
        store.start()
        stores.append(store)
    for start in range(0, width, 256):
        columns = slice(start, start + 256)
        normed[total:, columns] = jnp.dot(
            select, normed[:total, columns], preferred_element_type=F32
        ).astype(BF16)
    multiply(normed, total, NGLOB, pair, results)
    gsum[...] = results[total:, :]
    if first:
        lane = lax.broadcasted_iota(jnp.int32, (1, rows), 1)
        own = (info.own_column() == lane).astype(BF16)
        for start in range(0, width, 256):
            columns = slice(start, start + 256)
            query = jnp.dot(
                normed[:rows, :], weight[2, :, columns], preferred_element_type=F32
            ).astype(BF16)
            queries[:, columns] = query
            gq_sets[0][:, columns] = jnp.dot(
                own, query, preferred_element_type=F32
            ).astype(BF16)
    tiles = info.tiles
    if kind == "middle":
        tiles = jnp.maximum(tiles, Globals(bucket, table, rows, 1).tiles)
    global_partial(tiles, gq_sets, results, total, scores, states)
    pairs = list(zip(states, kept))
    move_state(tiles, pairs, sems, "start")
    move_state(tiles, pairs, sems, "wait")
    for store in stores:
        store.wait()


def call(kernel, inputs, specs, outs, out_specs, scratch, name, cost=COST):
    return pl.pallas_call(
        kernel,
        out_shape=[jax.ShapeDtypeStruct(*out) for out in outs],
        in_specs=specs,
        out_specs=out_specs,
        scratch_shapes=scratch,
        compiler_params=params(LIMIT),
        cost_estimate=cost,
        name=name,
    )(*inputs)


def rows_call(shards, places, kind, index, gain, pieces, weights, *more):
    rows, width = pieces[0].shape
    count = len(pieces)
    first = kind == "first"
    sets = 2 if kind == "middle" else 1
    total = count * rows
    outs = [((total, 2 * width), BF16), ((NGLOB, 2 * width), BF16)]
    outs += [((3, NGLOB, width), F32)] * sets
    specs = [HBM, VMEM] + [HBM] * sets
    if first:
        outs += [((rows, width), BF16), ((NGLOB, width), BF16)]
        specs += [VMEM, VMEM]
    scratch = [
        pltpu.VMEM((count, rows, width), BF16),
        pltpu.VMEM((len(weights), width, width), BF16),
        pltpu.VMEM((total + NGLOB, width), BF16),
        pltpu.VMEM((total + NGLOB, 2 * width), BF16),
        pltpu.SemaphoreType.DMA((count,)),
        pltpu.SemaphoreType.DMA((len(weights),)),
        pltpu.SemaphoreType.DMA((total // CHUNK,)),
        pltpu.SemaphoreType.DMA((NGLOB // TILE, sets)),
        pltpu.VMEM((sets * GROUP * TILE, total), F32),
    ] + [pltpu.VMEM((3, NGLOB, width), F32)] * sets
    return call(
        functools.partial(rows_kernel, shards, places, kind),
        [*index, gain, *pieces, *weights, *more],
        [SMEM, VMEM, VMEM] + [HBM] * (count + len(weights)) + [VMEM] * len(more),
        outs,
        specs,
        scratch,
        kind,
        LATE_COST if kind == "late" else COST,
    )


def pick_table(random_blocks, rows, shards):
    me = lax.axis_index("seq").astype(jnp.int32)
    blocks = rows // BLOCK
    steps = shards // 2
    total = shards * blocks
    here = me * blocks + jnp.arange(blocks, dtype=jnp.int32)[:, None]
    window = lax.rem(here + total + jnp.arange(-1, 2, dtype=jnp.int32)[None, :], total)
    listed = lax.dynamic_slice_in_dim(random_blocks.astype(jnp.int32), me * blocks, blocks, 0)
    chosen = jnp.concatenate([window, listed], axis=1).reshape(-1)
    device = chosen // blocks
    step, core = place_of(device, me, shards)
    edge = (step == 0) | (step == steps - 1)
    piece = jnp.where(edge, core, step - 1)
    source = jnp.where(step == 0, 0, jnp.where(edge, 3, 1 + core))
    return source, piece * rows + (chosen - device * blocks) * BLOCK


def attend_kernel(shards, *refs):
    bucket, table, source_ref, start_ref, query_source, *g_sources, out_weight = refs[:10]
    part_refs = refs[10:14]
    kv_refs = refs[14:18]
    (out, queries, weight, tails, keys, mixed, placed, olds, result) = refs[18:27]
    sems, state_sems, load_sems, out_sems = refs[27:]
    rows, width = queries.shape
    blocks = rows // BLOCK
    span = PICKS * BLOCK
    info = Globals(bucket, table, rows)

    def copies(block, slot, act):
        for pick in range(PICKS):
            target = keys.at[slot, pl.ds(pick * BLOCK, BLOCK), :]
            sem = sems.at[slot, pick]
            if act == "wait":
                pltpu.make_async_copy(kv_refs[0].at[pl.ds(0, BLOCK), :], target, sem).wait()
                continue
            entry = block * PICKS + pick
            source = source_ref[entry]
            start = pl.multiple_of(start_ref[entry], BLOCK)
            for index, held in enumerate(kv_refs):

                @pl.when(source == index)
                def _():
                    pltpu.make_async_copy(held.at[pl.ds(start, BLOCK), :], target, sem).start()

    copies(0, 0, "start")
    loads = start_loads(
        [query_source, *g_sources, out_weight],
        [queries, *[tails.at[i] for i in range(4)], weight],
        load_sems,
    )
    mine_refs = [olds.at[i] for i in range(4)]
    pairs = list(zip(part_refs, mine_refs))
    move_state(info.tiles, pairs, state_sems, "start")
    placed[...] = jnp.zeros_like(placed)
    for load in loads[:5]:
        load.wait()
    gathered = (tails[0] + tails[1]) + (tails[2] + tails[3])
    keys[0, span:, :] = gathered
    keys[1, span:, :] = gathered

    def one_block(block, carry):
        slot = lax.rem(block, 2)

        @pl.when(block + 1 < blocks)
        def _():
            copies(block + 1, 1 - slot, "start")

        copies(block, slot, "wait")
        at = pl.ds(pl.multiple_of(block * BLOCK, BLOCK), BLOCK)
        groups = range(width // GW)
        score = [
            contract_last(
                spread_heads(queries[at, g * GW : (g + 1) * GW]),
                keys[slot, :, g * GW : (g + 1) * GW],
            )
            for g in groups
        ]
        probs = []
        totals = []
        for g in groups:
            top = jnp.max(score[g], axis=1, keepdims=True)
            prob = jnp.exp2((score[g] - top) * EXP2)
            totals.append(jnp.sum(prob, axis=1, keepdims=True))
            probs.append(prob.astype(BF16))
        for g in groups:
            weighted = jnp.dot(
                probs[g],
                keys[slot, :, width + g * GW : width + (g + 1) * GW],
                preferred_element_type=F32,
            )
            mixed[at, g * GW : (g + 1) * GW] = pick_heads(
                weighted * (1.0 / totals[g]), BLOCK
            ).astype(BF16)
        return carry

    lax.fori_loop(0, blocks, one_block, 0)
    move_state(info.tiles, pairs, state_sems, "wait")
    merge_states(info.tiles, mine_refs, placed)
    row = lax.broadcasted_iota(jnp.int32, (rows, NGLOB), 0)
    select = row == info.own_row()
    owned = jnp.max(select.astype(F32), axis=1, keepdims=True) > 0.5
    select = select.astype(BF16)
    for column in range(0, width, 256):
        columns = slice(column, column + 256)
        moved = jnp.dot(select, placed[:, columns], preferred_element_type=F32).astype(BF16)
        mixed[:, columns] = jnp.where(owned, moved, mixed[:, columns])
    loads[5].wait()
    for column in range(0, width, 256):
        columns = slice(column, column + 256)
        result[:, columns] = jnp.dot(
            mixed[...], weight[:, columns], preferred_element_type=F32
        ).astype(BF16)
        pltpu.make_async_copy(
            result.at[:, columns], out.at[:, columns], out_sems.at[column // 256]
        ).start()
    for column in range(0, width, 256):
        columns = slice(column, column + 256)
        pltpu.make_async_copy(
            result.at[:, columns], out.at[:, columns], out_sems.at[column // 256]
        ).wait()


def attend_call(shards, index, picks, queries, gsums, out_weight, parts, kv):
    rows, width = queries.shape
    keys = PICKS * BLOCK + NGLOB
    return call(
        functools.partial(attend_kernel, shards),
        [*index, *picks, queries, *gsums, out_weight, *parts, *kv],
        [SMEM, VMEM, SMEM, SMEM] + [HBM] * 14,
        [((rows, width), BF16)],
        [HBM],
        [
            pltpu.VMEM((rows, width), BF16),
            pltpu.VMEM((width, width), BF16),
            pltpu.VMEM((4, NGLOB, 2 * width), BF16),
            pltpu.VMEM((2, keys, 2 * width), BF16),
            pltpu.VMEM((rows, width), BF16),
            pltpu.VMEM((NGLOB, width), BF16),
            pltpu.VMEM((4, 3, NGLOB, width), F32),
            pltpu.VMEM((rows, width), BF16),
            pltpu.SemaphoreType.DMA((2, PICKS)),
            pltpu.SemaphoreType.DMA((NGLOB // TILE, 4)),
            pltpu.SemaphoreType.DMA((6,)),
            pltpu.SemaphoreType.DMA((width // 256,)),
        ],
        "attend",
    )[0]


def exchange(value, even, odd):
    count = lax.axis_size("seq")
    return lax.ppermute(value, "seq", [(i, i ^ (odd if i & 1 else even)) for i in range(count)])


def body(
    tokens,
    norm_gain,
    query_weight,
    key_weight,
    value_weight,
    out_weight,
    random_blocks,
    bucket_id,
    global_positions,
):
    shards = lax.axis_size("seq")
    width = tokens.shape[1]
    gain = norm_gain.reshape(1, width)
    pair = [key_weight, value_weight]
    index = [bucket_id, global_positions]
    steps = shards // 2
    if shards == 8:
        arrived = [tokens, exchange(tokens, 2, 4), exchange(tokens, 4, 2), None]
    else:
        arrived = [tokens] + [None] * (steps - 1)
        bit = 1
        while bit < steps:
            for step in range(bit):
                arrived[step | bit] = exchange(arrived[step], 2 * bit, 2 * bit)
            bit *= 2
    across = exchange(tokens, 1, 1)
    kv_own, g_first, s_first, queries, gq = rows_call(
        shards, [(0, 0), (0, 1)], "first", index, gain, [tokens, across], [*pair, query_weight]
    )
    gother = exchange(gq, 1, 1)
    picks = pick_table(random_blocks, tokens.shape[0], shards)
    kv_own, picks, *arrived[1:-1] = lax.optimization_barrier((kv_own, picks, *arrived[1:-1]))
    if shards == 8:
        arrived[3] = exchange(arrived[1], 4, 2)
    kv_mine, g_mine, s_mine, s_other = rows_call(
        shards,
        [(s, 0) for s in range(1, steps - 1)],
        "middle",
        index,
        gain,
        arrived[1:-1],
        pair,
        gq,
        gother,
    )
    kv_other, g_other = exchange(kv_mine, 1, 1), exchange(g_mine, 1, 1)
    s_mine, fresh = lax.optimization_barrier((s_mine, arrived[-1]))
    s_other = exchange(s_other, 1, 1)
    kv_late, g_late, s_late = rows_call(
        shards,
        [(steps - 1, 0), (steps - 1, 1)],
        "late",
        index,
        gain,
        [fresh, exchange(fresh, 1, 1)],
        pair,
        gq,
    )
    return attend_call(
        shards,
        index,
        picks,
        queries,
        [g_first, g_mine, g_other, g_late],
        out_weight,
        [s_first, s_mine, s_other, s_late],
        [kv_own, kv_mine, kv_other, kv_late],
    )


def solution(mesh):
    placed = (P(("dp", "seq"), None), P(), P(), P(), P(), P(), P("dp", None), P(), P())
    return jax.shard_map(
        body, mesh=mesh, in_specs=placed, out_specs=P(("dp", "seq"), None), check_vma=False
    )
```

```python
import functools
import math

import jax
import jax.numpy as jnp
from jax import lax
from jax.experimental import pallas as pl
from jax.experimental.pallas import tpu as pltpu
from jax.sharding import PartitionSpec as P

HEADS = 16
HDIM = 64
BLOCK = 64
RAND = 3
NGLOB = 128
GROUP = 4
GW = GROUP * HDIM
TILE = 32
CHUNK = 256
PICKS = 3 + RAND
EXP2 = HDIM ** (-0.5) * math.log2(math.e)
F32 = jnp.float32
BF16 = jnp.bfloat16
HBM = pl.BlockSpec(memory_space=pltpu.HBM)
VMEM = pl.BlockSpec(memory_space=pltpu.VMEM)
SMEM = pl.BlockSpec(memory_space=pltpu.SMEM)
LATE_COST = pl.CostEstimate(flops=10**11, bytes_accessed=1024, transcendentals=0)
COST = pl.CostEstimate(flops=1024, bytes_accessed=1024, transcendentals=0)


def params(mib):
    return pltpu.CompilerParams(vmem_limit_bytes=mib << 20)


LIMIT = 60


def hops_of(shards):
    if shards == 8:
        return [(0, 0), (2, 4), (4, 2), (6, 6)]
    return [(2 * step, 2 * step) for step in range(shards // 2)]


def layer_norm(tokens, gain):
    values = tokens.astype(F32)
    center = values - jnp.mean(values, axis=-1, keepdims=True)
    spread = jnp.mean(center * center, axis=-1, keepdims=True)
    return (center * lax.rsqrt(spread + 1e-05) * gain).astype(BF16)


def head_lane(rows):
    return lax.broadcasted_iota(jnp.int32, (rows, GW), 1) // HDIM


def spread_heads(rows):
    lane = head_lane(rows.shape[0])
    masks = [(lane == head).astype(BF16) for head in range(GROUP)]
    return jnp.concatenate([rows * mask for mask in masks], axis=0)


def pick_heads(stacked, rows):
    lane = head_lane(rows)
    picked = stacked[(GROUP - 1) * rows :]
    for head in range(GROUP - 1):
        picked = jnp.where(lane == head, stacked[head * rows : (head + 1) * rows], picked)
    return picked


def contract_last(left, right):
    return lax.dot_general(left, right, (((1,), (1,)), ((), ())), preferred_element_type=F32)


def square(axis):
    return lax.broadcasted_iota(jnp.int32, (NGLOB, NGLOB), axis)


class Globals:
    def __init__(self, bucket, table, rows, core=0):
        self.me = lax.axis_index("seq") ^ core
        self.rows = rows
        self.row = table[pl.ds(bucket[0], 1), :]
        self.local = self.row - self.me * rows
        self.first = jnp.sum((self.local < 0).astype(F32)).astype(jnp.int32)
        below = jnp.sum((self.local < rows).astype(F32)).astype(jnp.int32)
        self.count = below - self.first
        self.tiles = (self.count + TILE - 1) // TILE

    def column(self):
        spread = jnp.where(square(0) == square(1), self.row, 0).astype(F32)
        return jnp.sum(spread, axis=1, keepdims=True).astype(jnp.int32)

    def own_column(self):
        hit = jnp.where(square(1) == square(0) + self.first, self.local, 0).astype(F32)
        found = jnp.sum(hit, axis=1, keepdims=True).astype(jnp.int32)
        index = lax.broadcasted_iota(jnp.int32, (NGLOB, 1), 0)
        return jnp.where(index < self.count, found, -1)

    def own_row(self):
        local = self.column() - self.me * self.rows
        hit = jnp.where(square(0) == square(1) + self.first, local, 0).astype(F32)
        found = jnp.sum(hit, axis=0, keepdims=True).astype(jnp.int32)
        index = lax.broadcasted_iota(jnp.int32, (1, NGLOB), 1)
        return jnp.where(index < self.count, found, -1)


def owner(me, step, core, shards):
    even, odd = hops_of(shards)[step]
    there = me ^ core
    return there ^ jnp.where(there & 1 == 0, even, odd)


def place_of(device, me, shards):
    slot = device ^ me
    core = slot & 1
    hop = slot - core
    if shards != 8:
        return hop // 2, core
    parity = (me ^ core) & 1
    near = jnp.where((hop == 2) == (parity == 0), 1, 2)
    return jnp.where(hop == 0, 0, jnp.where(hop == 6, 3, near)), core


def start_loads(sources, targets, sems):
    loads = []
    for index, (source, target) in enumerate(zip(sources, targets)):
        load = pltpu.make_async_copy(source, target, sems.at[index])
        load.start()
        loads.append(load)
    return loads


def select_rows(info, bases, rows):
    lane = lax.broadcasted_iota(jnp.int32, (1, len(bases) * rows), 1)
    column = info.column()
    where = jnp.full((NGLOB, 1), -1, jnp.int32)
    for piece, base in enumerate(bases):
        inside = column - base * rows
        hit = jnp.where(inside < 0, rows, inside) < rows
        where = jnp.where(hit, inside + piece * rows, where)
    return (where == lane).astype(BF16)


def norm_chunk(tokens, gain, normed, at):
    rows = tokens.shape[1]
    piece, start = at // rows, at % rows
    for row in range(0, CHUNK, 64):
        normed[at + row : at + row + 64, :] = layer_norm(
            tokens[piece, start + row : start + row + 64, :], gain[...]
        )


def multiply(normed, at, height, weights, results):
    left = normed[at : at + height, :]
    width = normed.shape[1]
    for index, weight in enumerate(weights):
        for start in range(0, width, 256):
            results[at : at + height, index * width + start : index * width + start + 256] = (
                jnp.dot(
                    left, weight[:, start : start + 256], preferred_element_type=F32
                ).astype(BF16)
            )


def global_partial(tiles, queries, kv, total, scores, states):
    width = queries[0].shape[1]
    stacked = GROUP * TILE
    count = len(queries)

    def one_tile(tile, carry):
        at = pl.ds(pl.multiple_of(tile * TILE, TILE), TILE)
        for group in range(width // GW):
            columns = slice(group * GW, (group + 1) * GW)
            values = slice(width + group * GW, width + (group + 1) * GW)
            left = [spread_heads(ref[at, columns]) for ref in queries]
            left = left[0] if count == 1 else jnp.concatenate(left, axis=0)
            scores[...] = contract_last(left, kv[:total, columns])
            top = jnp.max(scores[...], axis=1, keepdims=True)
            probs = jnp.exp2((scores[...] - top) * EXP2)
            part = jnp.sum(probs, axis=1, keepdims=True)
            acc = jnp.dot(probs.astype(BF16), kv[:total, values], preferred_element_type=F32)
            shape = (count * stacked, GW)
            for index, value in enumerate(
                (jnp.broadcast_to(top, shape), jnp.broadcast_to(part, shape), acc)
            ):
                for which, state in enumerate(states):
                    state[index, at, columns] = pick_heads(
                        value[which * stacked : (which + 1) * stacked], TILE
                    )
        return carry

    lax.fori_loop(0, tiles, one_tile, 0)


def move_state(tiles, pairs, sems, act):
    for tile in range(NGLOB // TILE):

        @pl.when(tile < tiles)
        def _():
            rows = slice(tile * TILE, (tile + 1) * TILE)
            for index, (source, target) in enumerate(pairs):
                copy = pltpu.make_async_copy(
                    source.at[:, rows, :], target.at[:, rows, :], sems.at[tile, index]
                )
                copy.start() if act == "start" else copy.wait()


def merge_states(tiles, states, target):
    def one_tile(tile, carry):
        at = pl.ds(pl.multiple_of(tile * TILE, TILE), TILE)
        top = functools.reduce(jnp.maximum, [ref[0, at, :] for ref in states])
        total = jnp.zeros_like(top)
        acc = jnp.zeros_like(top)
        for ref in states:
            factor = jnp.exp2((ref[0, at, :] - top) * EXP2)
            total += ref[1, at, :] * factor
            acc += ref[2, at, :] * factor
        target[at, :] = (acc / total).astype(BF16)
        return carry

    lax.fori_loop(0, tiles, one_tile, 0)


def rows_kernel(shards, places, kind, *refs):
    count = len(places)
    first = kind == "first"
    sets = 2 if kind == "middle" else 1
    refs = list(refs)

    def take(number):
        taken = refs[:number]
        del refs[:number]
        return taken

    bucket, table, gain = take(3)
    sources = take(count)
    weights = take(2 + first)
    gq_sets = take(0 if first else sets)
    out, gsum = take(2)
    kept = take(sets)
    if first:
        (queries,) = take(1)
        gq_sets = take(1)
    tokens, weight, normed, results, token_sems, weight_sems, out_sems, sems, scores = take(9)
    states = take(sets)
    rows, width = sources[0].shape
    total = count * rows
    loads = start_loads(sources, [tokens.at[i] for i in range(count)], token_sems)
    arrivals = start_loads(weights, [weight.at[i] for i in range(len(weights))], weight_sems)
    info = Globals(bucket, table, rows)
    bases = [owner(info.me, step, core, shards) for step, core in places]
    select = select_rows(info, bases, rows)
    loads[0].wait()
    norm_chunk(tokens, gain, normed, 0)
    for load in loads[1:] + arrivals:
        load.wait()
    pair = [weight.at[0], weight.at[1]]
    stores = []
    for at in range(0, total, CHUNK):
        if at + CHUNK < total:
            norm_chunk(tokens, gain, normed, at + CHUNK)
        multiply(normed, at, CHUNK, pair, results)
        store = pltpu.make_async_copy(
            results.at[at : at + CHUNK, :], out.at[at : at + CHUNK, :], out_sems.at[at // CHUNK]
        )
        store.start()
        stores.append(store)
    for start in range(0, width, 256):
        columns = slice(start, start + 256)
        normed[total:, columns] = jnp.dot(
            select, normed[:total, columns], preferred_element_type=F32
        ).astype(BF16)
    multiply(normed, total, NGLOB, pair, results)
    gsum[...] = results[total:, :]
    if first:
        lane = lax.broadcasted_iota(jnp.int32, (1, rows), 1)
        own = (info.own_column() == lane).astype(BF16)
        for start in range(0, width, 256):
            columns = slice(start, start + 256)
            query = jnp.dot(
                normed[:rows, :], weight[2, :, columns], preferred_element_type=F32
            ).astype(BF16)
            queries[:, columns] = query
            gq_sets[0][:, columns] = jnp.dot(
                own, query, preferred_element_type=F32
            ).astype(BF16)
    tiles = info.tiles
    if kind == "middle":
        tiles = jnp.maximum(tiles, Globals(bucket, table, rows, 1).tiles)
    global_partial(tiles, gq_sets, results, total, scores, states)
    pairs = list(zip(states, kept))
    move_state(tiles, pairs, sems, "start")
    move_state(tiles, pairs, sems, "wait")
    for store in stores:
        store.wait()


def call(kernel, inputs, specs, outs, out_specs, scratch, name, cost=COST):
    return pl.pallas_call(
        kernel,
        out_shape=[jax.ShapeDtypeStruct(*out) for out in outs],
        in_specs=specs,
        out_specs=out_specs,
        scratch_shapes=scratch,
        compiler_params=params(LIMIT),
        cost_estimate=cost,
        name=name,
    )(*inputs)


def rows_call(shards, places, kind, index, gain, pieces, weights, *more):
    rows, width = pieces[0].shape
    count = len(pieces)
    first = kind == "first"
    sets = 2 if kind == "middle" else 1
    total = count * rows
    outs = [((total, 2 * width), BF16), ((NGLOB, 2 * width), BF16)]
    outs += [((3, NGLOB, width), F32)] * sets
    specs = [HBM, VMEM] + [HBM] * sets
    if first:
        outs += [((rows, width), BF16), ((NGLOB, width), BF16)]
        specs += [VMEM, VMEM]
    scratch = [
        pltpu.VMEM((count, rows, width), BF16),
        pltpu.VMEM((len(weights), width, width), BF16),
        pltpu.VMEM((total + NGLOB, width), BF16),
        pltpu.VMEM((total + NGLOB, 2 * width), BF16),
        pltpu.SemaphoreType.DMA((count,)),
        pltpu.SemaphoreType.DMA((len(weights),)),
        pltpu.SemaphoreType.DMA((total // CHUNK,)),
        pltpu.SemaphoreType.DMA((NGLOB // TILE, sets)),
        pltpu.VMEM((sets * GROUP * TILE, total), F32),
    ] + [pltpu.VMEM((3, NGLOB, width), F32)] * sets
    return call(
        functools.partial(rows_kernel, shards, places, kind),
        [*index, gain, *pieces, *weights, *more],
        [SMEM, VMEM, VMEM] + [HBM] * (count + len(weights)) + [VMEM] * len(more),
        outs,
        specs,
        scratch,
        kind,
        LATE_COST if kind == "late" else COST,
    )


def pick_table(random_blocks, rows, shards):
    me = lax.axis_index("seq").astype(jnp.int32)
    blocks = rows // BLOCK
    steps = shards // 2
    total = shards * blocks
    here = me * blocks + jnp.arange(blocks, dtype=jnp.int32)[:, None]
    window = lax.rem(here + total + jnp.arange(-1, 2, dtype=jnp.int32)[None, :], total)
    listed = lax.dynamic_slice_in_dim(random_blocks.astype(jnp.int32), me * blocks, blocks, 0)
    chosen = jnp.concatenate([window, listed], axis=1).reshape(-1)
    device = chosen // blocks
    step, core = place_of(device, me, shards)
    edge = (step == 0) | (step == steps - 1)
    piece = jnp.where(edge, core, step - 1)
    source = jnp.where(step == 0, 0, jnp.where(edge, 3, 1 + core))
    return source, piece * rows + (chosen - device * blocks) * BLOCK


def attend_kernel(shards, *refs):
    bucket, table, source_ref, start_ref, query_source, *g_sources, out_weight = refs[:10]
    part_refs = refs[10:14]
    kv_refs = refs[14:18]
    (out, queries, weight, tails, keys, mixed, placed, olds, result) = refs[18:27]
    sems, state_sems, load_sems, out_sems = refs[27:]
    rows, width = queries.shape
    blocks = rows // BLOCK
    span = PICKS * BLOCK
    info = Globals(bucket, table, rows)

    def copies(block, slot, act):
        for pick in range(PICKS):
            target = keys.at[slot, pl.ds(pick * BLOCK, BLOCK), :]
            sem = sems.at[slot, pick]
            if act == "wait":
                pltpu.make_async_copy(kv_refs[0].at[pl.ds(0, BLOCK), :], target, sem).wait()
                continue
            entry = block * PICKS + pick
            source = source_ref[entry]
            start = pl.multiple_of(start_ref[entry], BLOCK)
            for index, held in enumerate(kv_refs):

                @pl.when(source == index)
                def _():
                    pltpu.make_async_copy(held.at[pl.ds(start, BLOCK), :], target, sem).start()

    copies(0, 0, "start")
    loads = start_loads(
        [query_source, *g_sources, out_weight],
        [queries, *[tails.at[i] for i in range(4)], weight],
        load_sems,
    )
    mine_refs = [olds.at[i] for i in range(4)]
    pairs = list(zip(part_refs, mine_refs))
    move_state(info.tiles, pairs, state_sems, "start")
    placed[...] = jnp.zeros_like(placed)
    for load in loads[:5]:
        load.wait()
    gathered = (tails[0] + tails[1]) + (tails[2] + tails[3])
    keys[0, span:, :] = gathered
    keys[1, span:, :] = gathered

    def one_block(block, carry):
        slot = lax.rem(block, 2)

        @pl.when(block + 1 < blocks)
        def _():
            copies(block + 1, 1 - slot, "start")

        copies(block, slot, "wait")
        at = pl.ds(pl.multiple_of(block * BLOCK, BLOCK), BLOCK)
        groups = range(width // GW)
        score = [
            contract_last(
                spread_heads(queries[at, g * GW : (g + 1) * GW]),
                keys[slot, :, g * GW : (g + 1) * GW],
            )
            for g in groups
        ]
        probs = []
        totals = []
        for g in groups:
            top = jnp.max(score[g], axis=1, keepdims=True)
            prob = jnp.exp2((score[g] - top) * EXP2)
            totals.append(jnp.sum(prob, axis=1, keepdims=True))
            probs.append(prob.astype(BF16))
        for g in groups:
            weighted = jnp.dot(
                probs[g],
                keys[slot, :, width + g * GW : width + (g + 1) * GW],
                preferred_element_type=F32,
            )
            mixed[at, g * GW : (g + 1) * GW] = pick_heads(
                weighted * (1.0 / totals[g]), BLOCK
            ).astype(BF16)
        return carry

    lax.fori_loop(0, blocks, one_block, 0)
    move_state(info.tiles, pairs, state_sems, "wait")
    merge_states(info.tiles, mine_refs, placed)
    row = lax.broadcasted_iota(jnp.int32, (rows, NGLOB), 0)
    select = row == info.own_row()
    owned = jnp.max(select.astype(F32), axis=1, keepdims=True) > 0.5
    select = select.astype(BF16)
    for column in range(0, width, 256):
        columns = slice(column, column + 256)
        moved = jnp.dot(select, placed[:, columns], preferred_element_type=F32).astype(BF16)
        mixed[:, columns] = jnp.where(owned, moved, mixed[:, columns])
    loads[5].wait()
    for column in range(0, width, 256):
        columns = slice(column, column + 256)
        result[:, columns] = jnp.dot(
            mixed[...], weight[:, columns], preferred_element_type=F32
        ).astype(BF16)
        pltpu.make_async_copy(
            result.at[:, columns], out.at[:, columns], out_sems.at[column // 256]
        ).start()
    for column in range(0, width, 256):
        columns = slice(column, column + 256)
        pltpu.make_async_copy(
            result.at[:, columns], out.at[:, columns], out_sems.at[column // 256]
        ).wait()


def attend_call(shards, index, picks, queries, gsums, out_weight, parts, kv):
    rows, width = queries.shape
    keys = PICKS * BLOCK + NGLOB
    return call(
        functools.partial(attend_kernel, shards),
        [*index, *picks, queries, *gsums, out_weight, *parts, *kv],
        [SMEM, VMEM, SMEM, SMEM] + [HBM] * 14,
        [((rows, width), BF16)],
        [HBM],
        [
            pltpu.VMEM((rows, width), BF16),
            pltpu.VMEM((width, width), BF16),
            pltpu.VMEM((4, NGLOB, 2 * width), BF16),
            pltpu.VMEM((2, keys, 2 * width), BF16),
            pltpu.VMEM((rows, width), BF16),
            pltpu.VMEM((NGLOB, width), BF16),
            pltpu.VMEM((4, 3, NGLOB, width), F32),
            pltpu.VMEM((rows, width), BF16),
            pltpu.SemaphoreType.DMA((2, PICKS)),
            pltpu.SemaphoreType.DMA((NGLOB // TILE, 4)),
            pltpu.SemaphoreType.DMA((6,)),
            pltpu.SemaphoreType.DMA((width // 256,)),
        ],
        "attend",
    )[0]


def exchange(value, even, odd):
    count = lax.axis_size("seq")
    return lax.ppermute(value, "seq", [(i, i ^ (odd if i & 1 else even)) for i in range(count)])


def body(
    tokens,
    norm_gain,
    query_weight,
    key_weight,
    value_weight,
    out_weight,
    random_blocks,
    bucket_id,
    global_positions,
):
    shards = lax.axis_size("seq")
    width = tokens.shape[1]
    gain = norm_gain.reshape(1, width)
    pair = [key_weight, value_weight]
    index = [bucket_id, global_positions]
    steps = shards // 2
    if shards == 8:
        arrived = [tokens, exchange(tokens, 2, 4), exchange(tokens, 4, 2), None]
    else:
        arrived = [tokens] + [None] * (steps - 1)
        bit = 1
        while bit < steps:
            for step in range(bit):
                arrived[step | bit] = exchange(arrived[step], 2 * bit, 2 * bit)
            bit *= 2
    across = exchange(tokens, 1, 1)
    kv_own, g_first, s_first, queries, gq = rows_call(
        shards, [(0, 0), (0, 1)], "first", index, gain, [tokens, across], [*pair, query_weight]
    )
    gother = exchange(gq, 1, 1)
    picks = pick_table(random_blocks, tokens.shape[0], shards)
    kv_own, picks, gother, *arrived[1:-1] = lax.optimization_barrier(
        (kv_own, picks, gother, *arrived[1:-1])
    )
    if shards == 8:
        arrived[3] = exchange(arrived[1], 4, 2)
    kv_mine, g_mine, s_mine, s_other = rows_call(
        shards,
        [(s, 0) for s in range(1, steps - 1)],
        "middle",
        index,
        gain,
        arrived[1:-1],
        pair,
        gq,
        gother,
    )
    kv_other, g_other = exchange(kv_mine, 1, 1), exchange(g_mine, 1, 1)
    s_mine, fresh = lax.optimization_barrier((s_mine, arrived[-1]))
    s_other = exchange(s_other, 1, 1)
    kv_late, g_late, s_late = rows_call(
        shards,
        [(steps - 1, 0), (steps - 1, 1)],
        "late",
        index,
        gain,
        [fresh, exchange(fresh, 1, 1)],
        pair,
        gq,
    )
    return attend_call(
        shards,
        index,
        picks,
        queries,
        [g_first, g_mine, g_other, g_late],
        out_weight,
        [s_first, s_mine, s_other, s_late],
        [kv_own, kv_mine, kv_other, kv_late],
    )


def solution(mesh):
    placed = (P(("dp", "seq"), None), P(), P(), P(), P(), P(), P("dp", None), P(), P())
    return jax.shard_map(
        body, mesh=mesh, in_specs=placed, out_specs=P(("dp", "seq"), None), check_vma=False
    )
```

```python
import functools
import math

import jax
import jax.numpy as jnp
from jax import lax
from jax.experimental import pallas as pl
from jax.experimental.pallas import tpu as pltpu
from jax.sharding import PartitionSpec as P

HEADS = 16
HDIM = 64
BLOCK = 64
RAND = 3
NGLOB = 128
GROUP = 4
GW = GROUP * HDIM
TILE = 32
CHUNK = 256
PICKS = 3 + RAND
EXP2 = HDIM ** (-0.5) * math.log2(math.e)
F32 = jnp.float32
BF16 = jnp.bfloat16
HBM = pl.BlockSpec(memory_space=pltpu.HBM)
VMEM = pl.BlockSpec(memory_space=pltpu.VMEM)
SMEM = pl.BlockSpec(memory_space=pltpu.SMEM)
LATE_COST = pl.CostEstimate(flops=10**11, bytes_accessed=1024, transcendentals=0)
COST = pl.CostEstimate(flops=1024, bytes_accessed=1024, transcendentals=0)


def params(mib):
    return pltpu.CompilerParams(vmem_limit_bytes=mib << 20)


LIMIT = 60


def hops_of(shards):
    if shards == 8:
        return [(0, 0), (2, 4), (4, 2), (6, 6)]
    return [(2 * step, 2 * step) for step in range(shards // 2)]


def layer_norm(tokens, gain):
    values = tokens.astype(F32)
    center = values - jnp.mean(values, axis=-1, keepdims=True)
    spread = jnp.mean(center * center, axis=-1, keepdims=True)
    return (center * lax.rsqrt(spread + 1e-05) * gain).astype(BF16)


def head_lane(rows):
    return lax.broadcasted_iota(jnp.int32, (rows, GW), 1) // HDIM


def spread_heads(rows):
    lane = head_lane(rows.shape[0])
    masks = [(lane == head).astype(BF16) for head in range(GROUP)]
    return jnp.concatenate([rows * mask for mask in masks], axis=0)


def pick_heads(stacked, rows):
    lane = head_lane(rows)
    picked = stacked[(GROUP - 1) * rows :]
    for head in range(GROUP - 1):
        picked = jnp.where(lane == head, stacked[head * rows : (head + 1) * rows], picked)
    return picked


def contract_last(left, right):
    return lax.dot_general(left, right, (((1,), (1,)), ((), ())), preferred_element_type=F32)


def square(axis):
    return lax.broadcasted_iota(jnp.int32, (NGLOB, NGLOB), axis)


class Globals:
    def __init__(self, bucket, table, rows, core=0):
        self.me = lax.axis_index("seq") ^ core
        self.rows = rows
        self.row = table[pl.ds(bucket[0], 1), :]
        self.local = self.row - self.me * rows
        self.first = jnp.sum((self.local < 0).astype(F32)).astype(jnp.int32)
        below = jnp.sum((self.local < rows).astype(F32)).astype(jnp.int32)
        self.count = below - self.first
        self.tiles = (self.count + TILE - 1) // TILE

    def column(self):
        spread = jnp.where(square(0) == square(1), self.row, 0).astype(F32)
        return jnp.sum(spread, axis=1, keepdims=True).astype(jnp.int32)

    def own_column(self):
        hit = jnp.where(square(1) == square(0) + self.first, self.local, 0).astype(F32)
        found = jnp.sum(hit, axis=1, keepdims=True).astype(jnp.int32)
        index = lax.broadcasted_iota(jnp.int32, (NGLOB, 1), 0)
        return jnp.where(index < self.count, found, -1)

    def own_row(self):
        local = self.column() - self.me * self.rows
        hit = jnp.where(square(0) == square(1) + self.first, local, 0).astype(F32)
        found = jnp.sum(hit, axis=0, keepdims=True).astype(jnp.int32)
        index = lax.broadcasted_iota(jnp.int32, (1, NGLOB), 1)
        return jnp.where(index < self.count, found, -1)


def owner(me, step, core, shards):
    even, odd = hops_of(shards)[step]
    there = me ^ core
    return there ^ jnp.where(there & 1 == 0, even, odd)


def place_of(device, me, shards):
    slot = device ^ me
    core = slot & 1
    hop = slot - core
    if shards != 8:
        return hop // 2, core
    parity = (me ^ core) & 1
    near = jnp.where((hop == 2) == (parity == 0), 1, 2)
    return jnp.where(hop == 0, 0, jnp.where(hop == 6, 3, near)), core


def start_loads(sources, targets, sems):
    loads = []
    for index, (source, target) in enumerate(zip(sources, targets)):
        load = pltpu.make_async_copy(source, target, sems.at[index])
        load.start()
        loads.append(load)
    return loads


def select_rows(info, bases, rows):
    lane = lax.broadcasted_iota(jnp.int32, (1, len(bases) * rows), 1)
    column = info.column()
    where = jnp.full((NGLOB, 1), -1, jnp.int32)
    for piece, base in enumerate(bases):
        inside = column - base * rows
        hit = jnp.where(inside < 0, rows, inside) < rows
        where = jnp.where(hit, inside + piece * rows, where)
    return (where == lane).astype(BF16)


def norm_chunk(tokens, gain, normed, at):
    rows = tokens.shape[1]
    piece, start = at // rows, at % rows
    for row in range(0, CHUNK, 64):
        normed[at + row : at + row + 64, :] = layer_norm(
            tokens[piece, start + row : start + row + 64, :], gain[...]
        )


def multiply(normed, at, height, weights, results):
    left = normed[at : at + height, :]
    width = normed.shape[1]
    for index, weight in enumerate(weights):
        for start in range(0, width, 256):
            results[at : at + height, index * width + start : index * width + start + 256] = (
                jnp.dot(
                    left, weight[:, start : start + 256], preferred_element_type=F32
                ).astype(BF16)
            )


def global_partial(tiles, queries, kv, total, scores, states):
    width = queries[0].shape[1]
    stacked = GROUP * TILE
    count = len(queries)

    def one_tile(tile, carry):
        at = pl.ds(pl.multiple_of(tile * TILE, TILE), TILE)
        for group in range(width // GW):
            columns = slice(group * GW, (group + 1) * GW)
            values = slice(width + group * GW, width + (group + 1) * GW)
            left = [spread_heads(ref[at, columns]) for ref in queries]
            left = left[0] if count == 1 else jnp.concatenate(left, axis=0)
            scores[...] = contract_last(left, kv[:total, columns])
            top = jnp.max(scores[...], axis=1, keepdims=True)
            probs = jnp.exp2((scores[...] - top) * EXP2)
            part = jnp.sum(probs, axis=1, keepdims=True)
            acc = jnp.dot(probs.astype(BF16), kv[:total, values], preferred_element_type=F32)
            shape = (count * stacked, GW)
            for index, value in enumerate(
                (jnp.broadcast_to(top, shape), jnp.broadcast_to(part, shape), acc)
            ):
                for which, state in enumerate(states):
                    state[index, at, columns] = pick_heads(
                        value[which * stacked : (which + 1) * stacked], TILE
                    )
        return carry

    lax.fori_loop(0, tiles, one_tile, 0)


def move_state(tiles, pairs, sems, act):
    for tile in range(NGLOB // TILE):

        @pl.when(tile < tiles)
        def _():
            rows = slice(tile * TILE, (tile + 1) * TILE)
            for index, (source, target) in enumerate(pairs):
                copy = pltpu.make_async_copy(
                    source.at[:, rows, :], target.at[:, rows, :], sems.at[tile, index]
                )
                copy.start() if act == "start" else copy.wait()


def merge_states(tiles, states, target):
    def one_tile(tile, carry):
        at = pl.ds(pl.multiple_of(tile * TILE, TILE), TILE)
        top = functools.reduce(jnp.maximum, [ref[0, at, :] for ref in states])
        total = jnp.zeros_like(top)
        acc = jnp.zeros_like(top)
        for ref in states:
            factor = jnp.exp2((ref[0, at, :] - top) * EXP2)
            total += ref[1, at, :] * factor
            acc += ref[2, at, :] * factor
        target[at, :] = (acc / total).astype(BF16)
        return carry

    lax.fori_loop(0, tiles, one_tile, 0)


def rows_kernel(shards, places, kind, *refs):
    count = len(places)
    first = kind == "first"
    sets = 2 if kind == "middle" else 1
    refs = list(refs)

    def take(number):
        taken = refs[:number]
        del refs[:number]
        return taken

    bucket, table, gain = take(3)
    sources = take(count)
    weights = take(2 + first)
    gq_sets = take(0 if first else sets)
    out, gsum = take(2)
    kept = take(sets)
    if first:
        (queries,) = take(1)
        gq_sets = take(1)
    tokens, weight, normed, results, token_sems, weight_sems, out_sems, sems, scores = take(9)
    states = take(sets)
    rows, width = sources[0].shape
    total = count * rows
    loads = start_loads(sources, [tokens.at[i] for i in range(count)], token_sems)
    arrivals = start_loads(weights, [weight.at[i] for i in range(len(weights))], weight_sems)
    info = Globals(bucket, table, rows)
    bases = [owner(info.me, step, core, shards) for step, core in places]
    select = select_rows(info, bases, rows)
    loads[0].wait()
    norm_chunk(tokens, gain, normed, 0)
    for load in loads[1:] + arrivals:
        load.wait()
    pair = [weight.at[0], weight.at[1]]
    stores = []
    for at in range(0, total, CHUNK):
        if at + CHUNK < total:
            norm_chunk(tokens, gain, normed, at + CHUNK)
        multiply(normed, at, CHUNK, pair, results)
        store = pltpu.make_async_copy(
            results.at[at : at + CHUNK, :], out.at[at : at + CHUNK, :], out_sems.at[at // CHUNK]
        )
        store.start()
        stores.append(store)
    for start in range(0, width, 256):
        columns = slice(start, start + 256)
        normed[total:, columns] = jnp.dot(
            select, normed[:total, columns], preferred_element_type=F32
        ).astype(BF16)
    multiply(normed, total, NGLOB, pair, results)
    gsum[...] = results[total:, :]
    if first:
        lane = lax.broadcasted_iota(jnp.int32, (1, rows), 1)
        own = (info.own_column() == lane).astype(BF16)
        for start in range(0, width, 256):
            columns = slice(start, start + 256)
            query = jnp.dot(
                normed[:rows, :], weight[2, :, columns], preferred_element_type=F32
            ).astype(BF16)
            queries[:, columns] = query
            gq_sets[0][:, columns] = jnp.dot(
                own, query, preferred_element_type=F32
            ).astype(BF16)
    tiles = info.tiles
    if kind == "middle":
        tiles = jnp.maximum(tiles, Globals(bucket, table, rows, 1).tiles)
    global_partial(tiles, gq_sets, results, total, scores, states)
    pairs = list(zip(states, kept))
    move_state(tiles, pairs, sems, "start")
    move_state(tiles, pairs, sems, "wait")
    for store in stores:
        store.wait()


def call(kernel, inputs, specs, outs, out_specs, scratch, name, cost=COST):
    return pl.pallas_call(
        kernel,
        out_shape=[jax.ShapeDtypeStruct(*out) for out in outs],
        in_specs=specs,
        out_specs=out_specs,
        scratch_shapes=scratch,
        compiler_params=params(LIMIT),
        cost_estimate=cost,
        name=name,
    )(*inputs)


def rows_call(shards, places, kind, index, gain, pieces, weights, *more):
    rows, width = pieces[0].shape
    count = len(pieces)
    first = kind == "first"
    sets = 2 if kind == "middle" else 1
    total = count * rows
    outs = [((total, 2 * width), BF16), ((NGLOB, 2 * width), BF16)]
    outs += [((3, NGLOB, width), F32)] * sets
    specs = [HBM, VMEM] + [HBM] * sets
    if first:
        outs += [((rows, width), BF16), ((NGLOB, width), BF16)]
        specs += [VMEM, VMEM]
    scratch = [
        pltpu.VMEM((count, rows, width), BF16),
        pltpu.VMEM((len(weights), width, width), BF16),
        pltpu.VMEM((total + NGLOB, width), BF16),
        pltpu.VMEM((total + NGLOB, 2 * width), BF16),
        pltpu.SemaphoreType.DMA((count,)),
        pltpu.SemaphoreType.DMA((len(weights),)),
        pltpu.SemaphoreType.DMA((total // CHUNK,)),
        pltpu.SemaphoreType.DMA((NGLOB // TILE, sets)),
        pltpu.VMEM((sets * GROUP * TILE, total), F32),
    ] + [pltpu.VMEM((3, NGLOB, width), F32)] * sets
    return call(
        functools.partial(rows_kernel, shards, places, kind),
        [*index, gain, *pieces, *weights, *more],
        [SMEM, VMEM, VMEM] + [HBM] * (count + len(weights)) + [VMEM] * len(more),
        outs,
        specs,
        scratch,
        kind,
        LATE_COST if kind == "late" else COST,
    )


def pick_table(random_blocks, rows, shards):
    me = lax.axis_index("seq").astype(jnp.int32)
    blocks = rows // BLOCK
    steps = shards // 2
    total = shards * blocks
    here = me * blocks + jnp.arange(blocks, dtype=jnp.int32)[:, None]
    window = lax.rem(here + total + jnp.arange(-1, 2, dtype=jnp.int32)[None, :], total)
    listed = lax.dynamic_slice_in_dim(random_blocks.astype(jnp.int32), me * blocks, blocks, 0)
    chosen = jnp.concatenate([window, listed], axis=1).reshape(-1)
    device = chosen // blocks
    step, core = place_of(device, me, shards)
    edge = (step == 0) | (step == steps - 1)
    piece = jnp.where(edge, core, step - 1)
    source = jnp.where(step == 0, 0, jnp.where(edge, 3, 1 + core))
    return source, piece * rows + (chosen - device * blocks) * BLOCK


def attend_kernel(shards, *refs):
    bucket, table, source_ref, start_ref, query_source, *g_sources, out_weight = refs[:10]
    part_refs = refs[10:14]
    kv_refs = refs[14:18]
    (out, queries, weight, tails, keys, mixed, placed, olds, result) = refs[18:27]
    sems, state_sems, load_sems, out_sems = refs[27:]
    rows, width = queries.shape
    blocks = rows // BLOCK
    span = PICKS * BLOCK
    info = Globals(bucket, table, rows)

    def copies(block, slot, act):
        for pick in range(PICKS):
            target = keys.at[slot, pl.ds(pick * BLOCK, BLOCK), :]
            sem = sems.at[slot, pick]
            if act == "wait":
                pltpu.make_async_copy(kv_refs[0].at[pl.ds(0, BLOCK), :], target, sem).wait()
                continue
            if pick == 1:
                own = pl.ds(pl.multiple_of(block * BLOCK, BLOCK), BLOCK)
                pltpu.make_async_copy(kv_refs[0].at[own, :], target, sem).start()
                continue
            entry = block * PICKS + pick
            source = source_ref[entry]
            start = pl.multiple_of(start_ref[entry], BLOCK)
            for index, held in enumerate(kv_refs):

                @pl.when(source == index)
                def _():
                    pltpu.make_async_copy(held.at[pl.ds(start, BLOCK), :], target, sem).start()

    copies(0, 0, "start")
    loads = start_loads(
        [query_source, *g_sources, out_weight],
        [queries, *[tails.at[i] for i in range(4)], weight],
        load_sems,
    )
    mine_refs = [olds.at[i] for i in range(4)]
    pairs = list(zip(part_refs, mine_refs))
    move_state(info.tiles, pairs, state_sems, "start")
    placed[...] = jnp.zeros_like(placed)
    for load in loads[:5]:
        load.wait()
    gathered = (tails[0] + tails[1]) + (tails[2] + tails[3])
    keys[0, span:, :] = gathered
    keys[1, span:, :] = gathered

    def one_block(block, slot):

        @pl.when(block + 1 < blocks)
        def _():
            copies(block + 1, 1 - slot, "start")

        copies(block, slot, "wait")
        at = pl.ds(pl.multiple_of(block * BLOCK, BLOCK), BLOCK)
        groups = range(width // GW)
        score = [
            contract_last(
                spread_heads(queries[at, g * GW : (g + 1) * GW]),
                keys[slot, :, g * GW : (g + 1) * GW],
            )
            for g in groups
        ]
        probs = []
        totals = []
        for g in groups:
            top = jnp.max(score[g], axis=1, keepdims=True)
            prob = jnp.exp2((score[g] - top) * EXP2)
            totals.append(jnp.sum(prob, axis=1, keepdims=True))
            probs.append(prob.astype(BF16))
        for g in groups:
            weighted = jnp.dot(
                probs[g],
                keys[slot, :, width + g * GW : width + (g + 1) * GW],
                preferred_element_type=F32,
            )
            mixed[at, g * GW : (g + 1) * GW] = pick_heads(
                weighted * (1.0 / totals[g]), BLOCK
            ).astype(BF16)

    def two_blocks(step, carry):
        one_block(2 * step, 0)
        one_block(2 * step + 1, 1)
        return carry

    lax.fori_loop(0, blocks // 2, two_blocks, 0)
    move_state(info.tiles, pairs, state_sems, "wait")
    merge_states(info.tiles, mine_refs, placed)
    row = lax.broadcasted_iota(jnp.int32, (rows, NGLOB), 0)
    select = row == info.own_row()
    owned = jnp.max(select.astype(F32), axis=1, keepdims=True) > 0.5
    select = select.astype(BF16)
    for column in range(0, width, 256):
        columns = slice(column, column + 256)
        moved = jnp.dot(select, placed[:, columns], preferred_element_type=F32).astype(BF16)
        mixed[:, columns] = jnp.where(owned, moved, mixed[:, columns])
    loads[5].wait()
    for column in range(0, width, 256):
        columns = slice(column, column + 256)
        result[:, columns] = jnp.dot(
            mixed[...], weight[:, columns], preferred_element_type=F32
        ).astype(BF16)
        pltpu.make_async_copy(
            result.at[:, columns], out.at[:, columns], out_sems.at[column // 256]
        ).start()
    for column in range(0, width, 256):
        columns = slice(column, column + 256)
        pltpu.make_async_copy(
            result.at[:, columns], out.at[:, columns], out_sems.at[column // 256]
        ).wait()


def attend_call(shards, index, picks, queries, gsums, out_weight, parts, kv):
    rows, width = queries.shape
    keys = PICKS * BLOCK + NGLOB
    return call(
        functools.partial(attend_kernel, shards),
        [*index, *picks, queries, *gsums, out_weight, *parts, *kv],
        [SMEM, VMEM, SMEM, SMEM] + [HBM] * 14,
        [((rows, width), BF16)],
        [HBM],
        [
            pltpu.VMEM((rows, width), BF16),
            pltpu.VMEM((width, width), BF16),
            pltpu.VMEM((4, NGLOB, 2 * width), BF16),
            pltpu.VMEM((2, keys, 2 * width), BF16),
            pltpu.VMEM((rows, width), BF16),
            pltpu.VMEM((NGLOB, width), BF16),
            pltpu.VMEM((4, 3, NGLOB, width), F32),
            pltpu.VMEM((rows, width), BF16),
            pltpu.SemaphoreType.DMA((2, PICKS)),
            pltpu.SemaphoreType.DMA((NGLOB // TILE, 4)),
            pltpu.SemaphoreType.DMA((6,)),
            pltpu.SemaphoreType.DMA((width // 256,)),
        ],
        "attend",
    )[0]


def exchange(value, even, odd):
    count = lax.axis_size("seq")
    return lax.ppermute(value, "seq", [(i, i ^ (odd if i & 1 else even)) for i in range(count)])


def body(
    tokens,
    norm_gain,
    query_weight,
    key_weight,
    value_weight,
    out_weight,
    random_blocks,
    bucket_id,
    global_positions,
):
    shards = lax.axis_size("seq")
    width = tokens.shape[1]
    gain = norm_gain.reshape(1, width)
    pair = [key_weight, value_weight]
    index = [bucket_id, global_positions]
    steps = shards // 2
    if shards == 8:
        arrived = [tokens, exchange(tokens, 2, 4), exchange(tokens, 4, 2), None]
    else:
        arrived = [tokens] + [None] * (steps - 1)
        bit = 1
        while bit < steps:
            for step in range(bit):
                arrived[step | bit] = exchange(arrived[step], 2 * bit, 2 * bit)
            bit *= 2
    across = exchange(tokens, 1, 1)
    kv_own, g_first, s_first, queries, gq = rows_call(
        shards, [(0, 0), (0, 1)], "first", index, gain, [tokens, across], [*pair, query_weight]
    )
    gother = exchange(gq, 1, 1)
    picks = pick_table(random_blocks, tokens.shape[0], shards)
    kv_own, picks, gother, *arrived[1:-1] = lax.optimization_barrier(
        (kv_own, picks, gother, *arrived[1:-1])
    )
    if shards == 8:
        arrived[3] = exchange(arrived[1], 4, 2)
    kv_mine, g_mine, s_mine, s_other = rows_call(
        shards,
        [(s, 0) for s in range(1, steps - 1)],
        "middle",
        index,
        gain,
        arrived[1:-1],
        pair,
        gq,
        gother,
    )
    kv_other, g_other = exchange(kv_mine, 1, 1), exchange(g_mine, 1, 1)
    s_mine, fresh = lax.optimization_barrier((s_mine, arrived[-1]))
    s_other = exchange(s_other, 1, 1)
    kv_late, g_late, s_late = rows_call(
        shards,
        [(steps - 1, 0), (steps - 1, 1)],
        "late",
        index,
        gain,
        [fresh, exchange(fresh, 1, 1)],
        pair,
        gq,
    )
    return attend_call(
        shards,
        index,
        picks,
        queries,
        [g_first, g_mine, g_other, g_late],
        out_weight,
        [s_first, s_mine, s_other, s_late],
        [kv_own, kv_mine, kv_other, kv_late],
    )


def solution(mesh):
    placed = (P(("dp", "seq"), None), P(), P(), P(), P(), P(), P("dp", None), P(), P())
    return jax.shard_map(
        body, mesh=mesh, in_specs=placed, out_specs=P(("dp", "seq"), None), check_vma=False
    )
```
